32 devices in a mesh: groups: 2 (over x), frame: 8 (over z, y), space: 2 (over core).
Axes of the slice: x: 2, y: 2, z: 4, core: 2. Of those that a mesh axis runs over, the one named last changes fastest.
Arguments:
- queries: bfloat16 [16, 12, 80, 2240], P(('groups', 'frame'), 'space'), parts along dimension 0, may hold values from -6 to 6
- keys: bfloat16 [16, 12, 80, 2240], P(('groups', 'frame'), 'space'), parts along dimension 0, may hold values from -6 to 6
- values: bfloat16 [16, 12, 80, 2240], P(('groups', 'frame'), 'space'), parts along dimension 0, may hold values from -6 to 6
- residual: bfloat16 [16, 12, 80, 2240], P(('groups', 'frame'), 'space'), parts along dimension 0, may hold values from -6 to 6
- attn_gain: float32 [2240], replicated, may hold values from 0.5 to 1.5
- value_taps: float32 [9, 2240], replicated, may hold values from -2 to 2
- gate_taps: float32 [9, 2240], replicated, may hold values from -2 to 2
Outputs:
- block_out: bfloat16 [16, 12, 80, 2240], P(('groups', 'frame'), 'space'), parts along dimension 0
The draws below stay inside these ranges and needn't reach their ends.
There are 2 independent parts, one for each index of `groups`. The reference program is written for one: setup_inputs(seed, part) draws one part's arguments, and reference() takes and returns one part's arrays. A program takes and returns all parts, laid end to end along the dimension named above; an argument that names none is the same for every part. Nothing has to cross between parts.
All inputs are finite; a program needn't handle non-finite values.
Results may differ from the reference program's by a relative error of at most 0.008.
Values may be sent and summed in bfloat16 or wider, within the bound.
A program may use at most 128 MiB of HBM per device.

```python
import jax
import jax.numpy as jnp
from jax import lax

D = 2240
HEADS = 20
HEAD_DIM = 112
WID = 80
HGT = 12
FRAMES = 8


def block_scale(rng, shape, cuts, smallest, top_value):
    level, own = 1.0, jax.random.fold_in(rng, 6)
    for position, blocks in cuts:
        draws = jnp.exp(jax.random.uniform(jax.random.fold_in(own, position), (blocks,), jnp.float32, smallest / len(cuts), top_value / len(cuts)))
        level = level * jnp.repeat(draws, shape[position] // blocks).reshape([-1 if axis == position else 1 for axis in range(len(shape))])
    return level


def normal_values(rng, dims, deviation, limit, split=(), held_as=jnp.bfloat16):
    loudness = block_scale(rng, dims, split, -0.22, 0.18) if split else 1.0
    array = jax.random.normal(rng, dims, jnp.float32) * deviation * loudness
    return jnp.minimum(jnp.maximum(array, -limit), limit).astype(held_as)


def setup_inputs(seed: int = 0, part: int = 0) -> dict:
    key_list = jax.random.split(jax.random.key(seed), 8)
    own_keys = jax.random.split(jax.random.fold_in(key_list[7], part), 8)
    queries = normal_values(own_keys[0], (FRAMES, HGT, WID, D), 1.0, 6.0, ((0, 8), (1, 2)))
    keys = normal_values(own_keys[1], (FRAMES, HGT, WID, D), 1.0, 6.0, ((0, 8), (1, 2)))
    values = normal_values(own_keys[2], (FRAMES, HGT, WID, D), 1.0, 6.0, ((0, 8), (1, 2)))
    residual = normal_values(own_keys[3], (FRAMES, HGT, WID, D), 1.0, 6.0, ((0, 8), (1, 2)))
    attn_gain = jnp.clip(1.0 + 0.1 * jax.random.normal(key_list[4], (D,), jnp.float32), 0.5, 1.5)
    value_taps = normal_values(key_list[5], (9, D), 9 ** -0.5, 2.0, (), jnp.float32)
    gate_taps = normal_values(key_list[6], (9, D), 9 ** -0.5, 2.0, (), jnp.float32)
    return {"queries": queries, "keys": keys, "values": values, "residual": residual, "attn_gain": attn_gain, "value_taps": value_taps, "gate_taps": gate_taps}


def reference(queries, keys, values, residual, attn_gain, value_taps, gate_taps):
    tokens = HGT * WID
    feature_keys = jnp.maximum(keys, 0).reshape(FRAMES, tokens, HEADS, HEAD_DIM).astype(jnp.float32)
    value_rows = values.reshape(FRAMES, tokens, HEADS, HEAD_DIM).astype(jnp.float32)
    own_state = jnp.einsum('fthk,fthv->fhkv', feature_keys, value_rows, precision=lax.Precision.HIGHEST)
    running = jnp.cumsum(own_state, axis=0)
    prev_state = jnp.concatenate([jnp.zeros_like(own_state[:1]), running[:-1] - 0.0 * own_state[:-1]], axis=0)
    prev_state = jnp.concatenate([jnp.zeros_like(own_state[:1]), jnp.cumsum(own_state, axis=0)[:-1]], axis=0)
    previous_frame_pass = prev_state.astype(jnp.bfloat16).astype(jnp.float32)
    local_frame_pass = own_state.astype(jnp.bfloat16).astype(jnp.float32)
    feature_queries = jnp.maximum(queries, 0).reshape(FRAMES, tokens, HEADS, HEAD_DIM).astype(jnp.float32)
    numerator_sum = jnp.einsum('fthk,fhkv->fthv', feature_queries, previous_frame_pass, precision=lax.Precision.HIGHEST)
    numerator_sum = numerator_sum + jnp.einsum('fthk,fhkv->fthv', feature_queries, local_frame_pass, precision=lax.Precision.HIGHEST)
    scale = lax.rsqrt(lax.optimization_barrier(jnp.mean(numerator_sum * numerator_sum, axis=-1, keepdims=True)) + 1e-06)
    normed = (numerator_sum * scale).reshape(FRAMES, HGT, WID, D)
    mixed = (residual.astype(jnp.float32) + normed * attn_gain).astype(jnp.bfloat16)
    padded = jnp.pad(mixed.astype(jnp.float32), ((0, 0), (1, 1), (1, 1), (0, 0)))
    conv_v = jnp.zeros((FRAMES, HGT, WID, D), jnp.float32)
    conv_g = jnp.zeros((FRAMES, HGT, WID, D), jnp.float32)
    for tap_row in range(3):
        for tap_col in range(3):
            window = padded[:, tap_row:tap_row + HGT, tap_col:tap_col + WID, :]
            conv_v = conv_v + value_taps[3 * tap_row + tap_col] * window
            conv_g = conv_g + gate_taps[3 * tap_row + tap_col] * window
    block_out = mixed.astype(jnp.float32) + conv_v * jax.nn.silu(conv_g)
    return block_out.astype(jnp.bfloat16)
```

```python
import functools

import jax
import jax.numpy as jnp
from jax import lax
from jax.experimental import pallas as pl
from jax.experimental.pallas import tpu as pltpu
from jax.sharding import PartitionSpec as P

HEAD_DIM = 112
LANES = 128
WINDOW = 256
PAD = 8
PIECE = 384
BLOCK = 384
PAIR = 2 * HEAD_DIM
LAG = 4
AHEAD = 2
F32, BF16 = jnp.float32, jnp.bfloat16


def windows(dim):
    out = []
    for lo in range(0, dim, WINDOW):
        w = min(WINDOW, dim - lo)
        h0, h1 = lo // HEAD_DIM, (lo + w - 1) // HEAD_DIM
        ks = HEAD_DIM * h0 // LANES * LANES
        ke = min(dim, -(-HEAD_DIM * (h1 + 1) // LANES) * LANES)
        out.append((lo, w, range(h0, h1 + 1), ks, ke))
    return out


def mix_kernel(
    frames, rows, width, dim,
    q_hbm, k_hbm, v_hbm, r_hbm, gain_ref, o_hbm,
    q, k, v, res, st, pb, rb, ob, yb, pr, ps, vb, qa, ra, ga, numer, sq, mixed,
    kv_sem, load_sem, edge_s, edge_r, rs_s, rs_r, y_s, y_r, z_s, z_r, pv_s, pv_r, out_sem,
):
    tokens = rows * width
    tiles = st.shape[0]
    space = lax.axis_index("space")
    frame = lax.axis_index("frame")
    other = 1 - space
    pair, odd = frame // 2, frame % 2
    twin = frame + 1 - 2 * odd
    has_prev = pair > 0
    has_next = pair < frames // 2 - 1
    wins = windows(dim)
    steps = len(wins)

    cuts = list(range(0, dim, PIECE)) + [dim]
    kv_loads = []
    for i, (lo, hi) in enumerate(zip(cuts, cuts[1:])):
        kv_loads.append(
            [
                pltpu.make_async_copy(src.at[:, lo:hi], dst.at[:, lo:hi], kv_sem.at[c, i])
                for c, (src, dst) in enumerate(((k_hbm, k), (v_hbm, v)))
            ]
        )
    loads = [
        pltpu.make_async_copy(src, dst.at[0:tokens], load_sem.at[i]) for i, (src, dst) in enumerate(((q_hbm, q), (r_hbm, res)))
    ]
    for copies in kv_loads:
        for copy in copies:
            copy.start()

    barrier = pltpu.get_barrier_semaphore()
    pl.semaphore_signal(barrier, inc=1, device_id={"space": other})
    pl.semaphore_signal(barrier, inc=1, device_id={"frame": twin})

    @pl.when(has_prev)
    def _():
        pl.semaphore_signal(barrier, inc=1, device_id={"frame": frame - 2})

    @pl.when(has_next)
    def _():
        pl.semaphore_signal(barrier, inc=1, device_id={"frame": frame + 2})

    st[tiles - 1] = jnp.zeros(st.shape[1:], F32)
    mixed[pl.ds(pl.multiple_of(space * (tokens + width), width), width), :] = jnp.zeros((width, dim), BF16)

    pl.semaphore_wait(barrier, 2 + jnp.where(has_prev, 1, 0) + jnp.where(has_next, 1, 0))

    def to_other(src, dst, tile, send, recv, j):
        return pltpu.make_async_remote_copy(
            src_ref=src.at[tile], dst_ref=dst.at[tile], send_sem=send.at[j], recv_sem=recv.at[j],
            device_id={"space": other},
        )

    def to_frame(src, dst, tile, send, recv, j, target):
        return pltpu.make_async_remote_copy(
            src_ref=src.at[tile], dst_ref=dst.at[tile], send_sem=send.at[j], recv_sem=recv.at[j],
            device_id={"frame": target},
        )

    edges = [
        pltpu.make_async_remote_copy(
            src_ref=src.at[pl.ds(pl.multiple_of(other * (tokens - width), width), width)],
            dst_ref=dst.at[tokens : tokens + width],
            send_sem=edge_s.at[i], recv_sem=edge_r.at[i], device_id={"space": other},
        )
        for i, (src, dst) in enumerate(((q_hbm, q), (r_hbm, res)))
    ]

    def head_of(lo, w):
        return (lax.broadcasted_iota(jnp.int32, (HEAD_DIM, w), 1) + lo) // HEAD_DIM

    def own_step(j):
        tile = 2 * j + space
        to_other(pb, rb, tile, rs_s, rs_r, j).wait_recv()
        total = st[tile] + rb[tile].astype(F32)
        st[tile] = total
        ob[tile] = total.astype(BF16)
        to_frame(ob, yb, tile, y_s, y_r, j, twin).start()

    ready = 0
    for m in range(steps):
        lo, w, heads, ks, ke = wins[m]
        while cuts[ready] < ke:
            for copy in kv_loads[ready]:
                copy.wait()
            ready += 1
            if ready == len(kv_loads):
                for copy in loads:
                    copy.start()
        full = lax.dot_general(
            jnp.maximum(k[:, ks:ke], 0), v[:, lo : lo + w], (((0,), (0,)), ((), ())), preferred_element_type=F32
        )
        owner = head_of(lo, w)
        slab = jnp.zeros((HEAD_DIM, w), F32)
        for h in heads:
            at = HEAD_DIM * h - ks
            slab = jnp.where(owner == h, full[at : at + HEAD_DIM, :], slab)
        for part in range(-(-w // LANES)):
            tile = lo // LANES + part
            wide = min(LANES, w - part * LANES)
            st[tile, :, :wide] = slab[:, part * LANES : part * LANES + wide]
            pb[tile] = st[tile].astype(BF16)
        to_other(pb, rb, 2 * m + other, rs_s, rs_r, m).start()
        if m >= LAG:
            own_step(m - LAG)
    for m in range(max(0, steps - LAG), steps):
        own_step(m)
    for copy in edges:
        copy.start()

    def scan_step(j):
        tile = 2 * j + space
        to_frame(ob, yb, tile, y_s, y_r, j, twin).wait_recv()
        beside = yb[tile].astype(F32)

        @pl.when(has_prev)
        def _():
            to_frame(ps, pr, tile, z_s, z_r, j, frame - 2).wait_recv()

        @pl.when(jnp.logical_not(has_prev))
        def _():
            pr[tile] = jnp.zeros(pr.shape[1:], BF16)

        before = pr[tile].astype(F32)

        @pl.when(has_next)
        def _():
            ps[tile] = (before + (st[tile] + beside)).astype(BF16)
            to_frame(ps, pr, tile, z_s, z_r, j, frame + 2).start()

        vb[tile] = (before + beside * odd.astype(F32) + st[tile]).astype(BF16)
        to_other(vb, vb, tile, pv_s, pv_r, j).start()

    pairs = dim // PAIR

    def realign(r0, r1):
        for j in range(pairs):
            qa[j, r0:r1, :PAIR] = jnp.maximum(q[r0:r1, PAIR * j : PAIR * (j + 1)], 0)
            ra[j, r0:r1, :PAIR] = res[r0:r1, PAIR * j : PAIR * (j + 1)]

    def cover(lo, hi, size):
        out = []
        while lo < hi:
            n = lo // size
            top = min(hi, size * (n + 1))
            out.append((n, lo - size * n, top - size * n))
            lo = top
        return out

    row_head = lax.broadcasted_iota(jnp.int32, (PAIR, PAIR), 0) < HEAD_DIM
    col_head = lax.broadcasted_iota(jnp.int32, (PAIR, PAIR), 1) < HEAD_DIM
    same = jnp.where(row_head == col_head, 1.0, 0.0).astype(BF16)
    first_head = lax.broadcasted_iota(jnp.int32, (HEAD_DIM, PAIR), 1) < HEAD_DIM

    def numer_step(j):
        parts = [vb[t, :, a:b] for t, a, b in cover(PAIR * j, PAIR * (j + 1), LANES)]
        slab = jnp.concatenate(parts, axis=1)
        zero = jnp.zeros_like(slab)
        both = jnp.concatenate([jnp.where(first_head, slab, zero), jnp.where(first_head, zero, slab)], axis=0)
        found = jnp.dot(qa[j, :, :PAIR], both, preferred_element_type=F32)
        numer[j % 3, :, :PAIR] = found
        sq[j % 3, :, :PAIR] = (found * found).astype(BF16)

    far = pl.ds(pl.multiple_of((1 - space) * (tokens + width), width), width)
    stores = []

    def mixed_step(j):
        total = jnp.dot(sq[j % 3, :, :PAIR], same, preferred_element_type=F32)
        scale = lax.rsqrt(total * (1.0 / HEAD_DIM) + 1e-6)
        normed = numer[j % 3, :, :PAIR] * scale
        qa[j, :, :PAIR] = (ra[j, :, :PAIR].astype(F32) + normed * ga[j : j + 1, :PAIR]).astype(BF16)
        t0, t1 = PAIR * j // LANES, PAIR * (j + 1) // LANES
        if j == pairs - 1:
            t1 = -(-dim // LANES)
        for t in range(t0, t1):
            lo, hi = LANES * t, min(dim, LANES * (t + 1))
            parts = [qa[n, :, a:b] for n, a, b in cover(lo, hi, PAIR)]
            value = jnp.concatenate(parts, axis=1) if len(parts) > 1 else parts[0]
            mixed[width : width + tokens, lo:hi] = value[:tokens]
            mixed[far, lo:hi] = value[tokens:]
        lo, hi = LANES * t0, min(dim, LANES * t1)
        store = pltpu.make_async_copy(mixed.at[:, lo:hi], o_hbm.at[:, lo:hi], out_sem.at[j])
        store.start()
        stores.append(store)

    for copy in loads:
        copy.wait()
    realign(0, tokens)
    for j in range(pairs):
        ga[j : j + 1, :PAIR] = gain_ref[0:1, PAIR * j : PAIR * (j + 1)]

    begun = 0
    for j in range(steps + AHEAD):
        if j < steps:
            scan_step(j)
        if j == AHEAD - 1:
            for copy in edges:
                copy.wait_recv()
            realign(tokens, tokens + width)
        m = j - AHEAD
        if m < 0:
            continue
        to_other(vb, vb, 2 * m + other, pv_s, pv_r, m).wait_recv()
        while begun < pairs and (PAIR * (begun + 1) - 1) // WINDOW <= m:
            numer_step(begun)
            if begun >= 2:
                mixed_step(begun - 2)
            begun += 1
    mixed_step(pairs - 2)
    mixed_step(pairs - 1)

    for copy in edges:
        copy.wait_send()

    def drain_step(j, _):
        mine, theirs = 2 * j + space, 2 * j + other
        to_other(pb, rb, theirs, rs_s, rs_r, j).wait_send()
        to_frame(ob, yb, mine, y_s, y_r, j, twin).wait_send()
        to_other(vb, vb, mine, pv_s, pv_r, j).wait_send()

        @pl.when(has_next)
        def _():
            to_frame(ps, pr, mine, z_s, z_r, j, frame + 2).wait_send()

        return 0

    lax.fori_loop(0, steps, drain_step, 0)
    for store in stores:
        store.wait()


def conv_kernel(rows, width, m_ref, vt_ref, gt_ref, o_ref, x32):
    step = width + 2 * PAD
    part = 16

    @pl.when(pl.program_id(0) == 0)
    def _():
        x32[...] = jnp.zeros_like(x32)

    def tile_step(t, _):
        at = pl.ds(pl.multiple_of(t * LANES, LANES), LANES)
        for row in range(rows + 2):
            x32[row * step + PAD : row * step + PAD + width, :] = m_ref[row * width : (row + 1) * width, at].astype(F32)
        taps = [
            (jnp.broadcast_to(vt_ref[n : n + 1, at], (part, LANES)), jnp.broadcast_to(gt_ref[n : n + 1, at], (part, LANES)))
            for n in range(9)
        ]
        for row in range(rows):
            for off in range(0, width, part):
                cv, cg = None, None
                for n in range(9):
                    start = (row + n // 3) * step + PAD - 1 + n % 3 + off
                    x = x32[start : start + part, :]
                    cv = taps[n][0] * x if cv is None else cv + taps[n][0] * x
                    cg = taps[n][1] * x if cg is None else cg + taps[n][1] * x
                centre = (row + 1) * step + PAD + off
                half = 0.5 * cg
                value = x32[centre : centre + part, :] + cv * (half + half * jnp.tanh(half))
                o_ref[row * width + off : row * width + off + part, at] = value.astype(BF16)
        return 0

    lax.fori_loop(0, o_ref.shape[1] // LANES, tile_step, 0)


def solution(mesh):
    frames = mesh.shape["frame"]

    def on_device(queries, keys, values, residual, attn_gain, value_taps, gate_taps):
        _, rows, width, dim = queries.shape
        tokens = rows * width
        steps = -(-dim // WINDOW)
        flat = lambda a: a.reshape(tokens, dim)
        anywhere = pl.BlockSpec(memory_space=pl.ANY)
        state = (2 * steps, HEAD_DIM, LANES)
        sems = pltpu.SemaphoreType.DMA((steps,))
        two = pltpu.SemaphoreType.DMA((2,))
        ext = tokens + width
        pairs = dim // PAIR
        mixed = pl.pallas_call(
            functools.partial(mix_kernel, frames, rows, width, dim),
            out_shape=jax.ShapeDtypeStruct((tokens + 2 * width, dim), BF16),
            in_specs=[anywhere] * 4 + [pl.BlockSpec(memory_space=pltpu.VMEM)],
            out_specs=anywhere,
            scratch_shapes=[
                pltpu.VMEM((ext, dim), BF16),
                pltpu.VMEM((tokens, dim), BF16),
                pltpu.VMEM((tokens, dim), BF16),
                pltpu.VMEM((ext, dim), BF16),
                pltpu.VMEM(state, F32),
            ]
            + [pltpu.VMEM(state, BF16)] * 7
            + [
                pltpu.VMEM((pairs, ext, WINDOW), BF16),
                pltpu.VMEM((pairs, ext, WINDOW), BF16),
                pltpu.VMEM((pairs, WINDOW), F32),
                pltpu.VMEM((3, ext, WINDOW), F32),
                pltpu.VMEM((3, ext, WINDOW), BF16),
                pltpu.VMEM((tokens + 2 * width, dim), BF16),
                pltpu.SemaphoreType.DMA((2, -(-dim // PIECE))),
                two,
                two,
                two,
            ]
            + [sems] * 8
            + [pltpu.SemaphoreType.DMA((pairs,))],
            compiler_params=pltpu.CompilerParams(collective_id=0, has_side_effects=True, vmem_limit_bytes=56 << 20),
        )(flat(queries), flat(keys), flat(values), flat(residual), attn_gain.reshape(1, dim))
        out = pl.pallas_call(
            functools.partial(conv_kernel, rows, width),
            out_shape=jax.ShapeDtypeStruct((tokens, dim), BF16),
            grid=(-(-dim // BLOCK),),
            in_specs=[
                pl.BlockSpec((tokens + 2 * width, BLOCK), lambda c: (0, c)),
                pl.BlockSpec((9, BLOCK), lambda c: (0, c)),
                pl.BlockSpec((9, BLOCK), lambda c: (0, c)),
            ],
            out_specs=pl.BlockSpec((tokens, BLOCK), lambda c: (0, c)),
            scratch_shapes=[pltpu.VMEM(((rows + 2) * (width + 2 * PAD), LANES), F32)],
        )(mixed, value_taps, gate_taps)
        return out.reshape(1, rows, width, dim)

    placed = P(("groups", "frame"), "space", None, None)
    return jax.shard_map(
        on_device,
        mesh=mesh,
        in_specs=(placed,) * 4 + (P(),) * 3,
        out_specs=placed,
        check_vma=False,
    )
```

```python
import functools

import jax
import jax.numpy as jnp
from jax import lax
from jax.experimental import pallas as pl
from jax.experimental.pallas import tpu as pltpu
from jax.sharding import PartitionSpec as P

HEAD_DIM = 112
LANES = 128
WINDOW = 256
PAD = 8
PIECE = 384
BLOCK = 384
PAIR = 2 * HEAD_DIM
LAG = 3
LEAD = 2
GROUP = 2
FETCH = 3
AHEAD = 2
F32, BF16 = jnp.float32, jnp.bfloat16


def windows(dim):
    out = []
    for lo in range(0, dim, WINDOW):
        w = min(WINDOW, dim - lo)
        h0, h1 = lo // HEAD_DIM, (lo + w - 1) // HEAD_DIM
        out.append((lo, w, range(h0, h1 + 1)))
    return out


def mix_kernel(
    frames, rows, width, dim,
    q_hbm, k_hbm, v_hbm, r_hbm, gain_ref, o_hbm,
    q, k, v, kt, res, st, pb, rb, ob, yb, pr, ps, vb, qa, ra, ga, numer, sq, mixed,
    kv_sem, load_sem, edge_s, edge_r, rs_s, rs_r, y_s, y_r, z_s, z_r, pv_s, pv_r, out_sem,
):
    tokens = rows * width
    tiles = st.shape[0]
    space = lax.axis_index("space")
    frame = lax.axis_index("frame")
    other = 1 - space
    pair, odd = frame // 2, frame % 2
    twin = frame + 1 - 2 * odd
    has_prev = pair > 0
    has_next = pair < frames // 2 - 1
    wins = windows(dim)
    steps = len(wins)

    cuts = list(range(0, dim, PIECE)) + [dim]
    kv_loads = []
    for i, (lo, hi) in enumerate(zip(cuts, cuts[1:])):
        kv_loads.append(
            [
                pltpu.make_async_copy(src.at[:, lo:hi], dst.at[:, lo:hi], kv_sem.at[c, i])
                for c, (src, dst) in enumerate(((k_hbm, k), (v_hbm, v)))
            ]
        )
    loads = [
        pltpu.make_async_copy(src, dst.at[0:tokens], load_sem.at[i]) for i, (src, dst) in enumerate(((q_hbm, q), (r_hbm, res)))
    ]
    for copies in kv_loads:
        for copy in copies:
            copy.start()

    barrier = pltpu.get_barrier_semaphore()
    pl.semaphore_signal(barrier, inc=1, device_id={"space": other})
    pl.semaphore_signal(barrier, inc=1, device_id={"frame": twin})

    @pl.when(has_prev)
    def _():
        pl.semaphore_signal(barrier, inc=1, device_id={"frame": frame - 2})

    @pl.when(has_next)
    def _():
        pl.semaphore_signal(barrier, inc=1, device_id={"frame": frame + 2})

    st[tiles - 1] = jnp.zeros(st.shape[1:], F32)
    mixed[pl.ds(pl.multiple_of(space * (tokens + width), width), width), :] = jnp.zeros((width, dim), BF16)

    def to_other(src, dst, tile, send, recv, j):
        return pltpu.make_async_remote_copy(
            src_ref=src.at[tile], dst_ref=dst.at[tile], send_sem=send.at[j], recv_sem=recv.at[j],
            device_id={"space": other},
        )

    def to_frame(src, dst, tile, send, recv, j, target):
        return pltpu.make_async_remote_copy(
            src_ref=src.at[tile], dst_ref=dst.at[tile], send_sem=send.at[j], recv_sem=recv.at[j],
            device_id={"frame": target},
        )

    edges = [
        pltpu.make_async_remote_copy(
            src_ref=src.at[pl.ds(pl.multiple_of(other * (tokens - width), width), width)],
            dst_ref=dst.at[tokens : tokens + width],
            send_sem=edge_s.at[i], recv_sem=edge_r.at[i], device_id={"space": other},
        )
        for i, (src, dst) in enumerate(((q_hbm, q), (r_hbm, res)))
    ]

    def head_of(lo, w):
        return (lax.broadcasted_iota(jnp.int32, (HEAD_DIM, w), 1) + lo) // HEAD_DIM

    def own_step(j):
        tile = 2 * j + space
        to_other(pb, rb, tile, rs_s, rs_r, j).wait_recv()
        total = st[tile] + rb[tile].astype(F32)
        st[tile] = total
        ob[tile] = total.astype(BF16)
        to_frame(ob, yb, tile, y_s, y_r, j, twin).start()

    ready, turned = 0, 0
    for m in range(steps):
        lo, w, heads = wins[m]
        k0, k1 = HEAD_DIM * heads[0], HEAD_DIM * (heads[-1] + 1)
        while cuts[ready] < max(k1, lo + w):
            for copy in kv_loads[ready]:
                copy.wait()
            ready += 1
        if m == FETCH:
            for copy in loads:
                copy.start()
        while turned < k1:
            top = min(dim, turned + LANES)
            kt[turned:top, :] = jnp.maximum(k[:, turned:top], 0).T
            turned = top
        full = jnp.dot(kt[k0:k1, :], v[:, lo : lo + w], preferred_element_type=F32)
        owner = head_of(lo, w)
        slab = full[:HEAD_DIM]
        for h in heads[1:]:
            at = HEAD_DIM * h - k0
            slab = jnp.where(owner == h, full[at : at + HEAD_DIM, :], slab)
        for part in range(-(-w // LANES)):
            tile = lo // LANES + part
            wide = min(LANES, w - part * LANES)
            st[tile, :, :wide] = slab[:, part * LANES : part * LANES + wide]
            pb[tile] = st[tile].astype(BF16)
        if m == LEAD - 1:
            pl.semaphore_wait(barrier, 2 + jnp.where(has_prev, 1, 0) + jnp.where(has_next, 1, 0))
        for n in range(m + 1) if m == LEAD - 1 else range(m, m + 1) if m >= LEAD else ():
            to_other(pb, rb, 2 * n + other, rs_s, rs_r, n).start()
        if m >= LAG:
            own_step(m - LAG)
    for m in range(max(0, steps - LAG), steps):
        own_step(m)
    for copy in edges:
        copy.start()

    def scan_step(j):
        tile = 2 * j + space
        to_frame(ob, yb, tile, y_s, y_r, j, twin).wait_recv()
        beside = yb[tile].astype(F32)

        @pl.when(has_prev)
        def _():
            to_frame(ps, pr, tile, z_s, z_r, j, frame - 2).wait_recv()

        @pl.when(jnp.logical_not(has_prev))
        def _():
            pr[tile] = jnp.zeros(pr.shape[1:], BF16)

        before = pr[tile].astype(F32)

        @pl.when(has_next)
        def _():
            ps[tile] = (before + (st[tile] + beside)).astype(BF16)
            to_frame(ps, pr, tile, z_s, z_r, j, frame + 2).start()

        vb[tile] = (before + beside * odd.astype(F32) + st[tile]).astype(BF16)
        to_other(vb, vb, tile, pv_s, pv_r, j).start()

    pairs = dim // PAIR

    def realign(r0, r1, j0, j1):
        for j in range(j0, min(j1, pairs)):
            qa[j, r0:r1, :PAIR] = jnp.maximum(q[r0:r1, PAIR * j : PAIR * (j + 1)], 0)
            ra[j, r0:r1, :PAIR] = res[r0:r1, PAIR * j : PAIR * (j + 1)]

    def cover(lo, hi, size):
        out = []
        while lo < hi:
            n = lo // size
            top = min(hi, size * (n + 1))
            out.append((n, lo - size * n, top - size * n))
            lo = top
        return out

    row_head = lax.broadcasted_iota(jnp.int32, (PAIR, PAIR), 0) < HEAD_DIM
    col_head = lax.broadcasted_iota(jnp.int32, (PAIR, PAIR), 1) < HEAD_DIM
    same = jnp.where(row_head == col_head, 1.0, 0.0).astype(BF16)
    first_head = lax.broadcasted_iota(jnp.int32, (HEAD_DIM, PAIR), 1) < HEAD_DIM

    def numer_step(j):
        parts = [vb[t, :, a:b] for t, a, b in cover(PAIR * j, PAIR * (j + 1), LANES)]
        slab = jnp.concatenate(parts, axis=1)
        zero = jnp.zeros_like(slab)
        both = jnp.concatenate([jnp.where(first_head, slab, zero), jnp.where(first_head, zero, slab)], axis=0)
        found = jnp.dot(qa[j, :, :PAIR], both, preferred_element_type=F32)
        numer[j % (2 * GROUP), :, :PAIR] = found
        sq[j % (2 * GROUP), :, :PAIR] = (found * found).astype(BF16)

    far = pl.ds(pl.multiple_of((1 - space) * (tokens + width), width), width)
    stores = []

    def mixed_step(j):
        total = jnp.dot(sq[j % (2 * GROUP), :, :PAIR], same, preferred_element_type=F32)
        scale = lax.rsqrt(total * (1.0 / HEAD_DIM) + 1e-6)
        normed = numer[j % (2 * GROUP), :, :PAIR] * scale
        qa[j, :, :PAIR] = (ra[j, :, :PAIR].astype(F32) + normed * ga[j : j + 1, :PAIR]).astype(BF16)
        t0, t1 = PAIR * j // LANES, PAIR * (j + 1) // LANES
        if j == pairs - 1:
            t1 = -(-dim // LANES)
        for t in range(t0, t1):
            lo, hi = LANES * t, min(dim, LANES * (t + 1))
            parts = [qa[n, :, a:b] for n, a, b in cover(lo, hi, PAIR)]
            value = jnp.concatenate(parts, axis=1) if len(parts) > 1 else parts[0]
            mixed[width : width + tokens, lo:hi] = value[:tokens]
            mixed[far, lo:hi] = value[tokens:]
        lo, hi = LANES * t0, min(dim, LANES * t1)
        store = pltpu.make_async_copy(mixed.at[:, lo:hi], o_hbm.at[:, lo:hi], out_sem.at[j])
        store.start()
        stores.append(store)

    for j in range(pairs):
        ga[j : j + 1, :PAIR] = gain_ref[PAIR * j : PAIR * (j + 1)].reshape(1, PAIR)

    def prepare(stage):
        if stage == 0:
            for copy in loads:
                copy.wait()
        if stage == 1:
            for copy in edges:
                copy.wait_recv()
            realign(tokens, tokens + width, 0, pairs)
        realign(0, tokens, 3 * stage, 3 * stage + 3)

    stages = -(-pairs // 3)

    @pl.when(has_prev)
    def _():
        for stage in range(stages):
            prepare(stage)

    begun = 0
    for j in range(steps + AHEAD):
        if j < steps:
            scan_step(j)
        if j < stages:
            @pl.when(jnp.logical_not(has_prev))
            def _():
                prepare(j)
        m = j - AHEAD
        if m < 0:
            continue
        to_other(vb, vb, 2 * m + other, pv_s, pv_r, m).wait_recv()
        while begun < pairs:
            until = min(pairs, begun + GROUP)
            if (PAIR * until - 1) // WINDOW > m:
                break
            for n in range(begun, until):
                numer_step(n)
            for n in range(max(0, begun - GROUP), begun):
                mixed_step(n)
            begun = until
    for n in range(max(0, pairs - GROUP) if pairs % GROUP == 0 else pairs - pairs % GROUP, pairs):
        mixed_step(n)

    for copy in edges:
        copy.wait_send()

    def drain_step(j, _):
        mine, theirs = 2 * j + space, 2 * j + other
        to_other(pb, rb, theirs, rs_s, rs_r, j).wait_send()
        to_frame(ob, yb, mine, y_s, y_r, j, twin).wait_send()
        to_other(vb, vb, mine, pv_s, pv_r, j).wait_send()

        @pl.when(has_next)
        def _():
            to_frame(ps, pr, mine, z_s, z_r, j, frame + 2).wait_send()

        return 0

    lax.fori_loop(0, steps, drain_step, 0)
    for store in stores:
        store.wait()


def conv_kernel(rows, width, m_ref, vt_ref, gt_ref, o_ref, x32):
    step = width + 2 * PAD
    part = 16

    @pl.when(pl.program_id(0) == 0)
    def _():
        x32[...] = jnp.zeros_like(x32)

    def tile_step(t, _):
        at = pl.ds(pl.multiple_of(t * LANES, LANES), LANES)
        for row in range(rows + 2):
            x32[row * step + PAD : row * step + PAD + width, :] = m_ref[row * width : (row + 1) * width, at].astype(F32)
        taps = [
            (jnp.broadcast_to(vt_ref[n : n + 1, at], (part, LANES)), jnp.broadcast_to(gt_ref[n : n + 1, at], (part, LANES)))
            for n in range(9)
        ]
        for row in range(rows):
            for off in range(0, width, part):
                cv, cg = None, None
                for n in range(9):
                    start = (row + n // 3) * step + PAD - 1 + n % 3 + off
                    x = x32[start : start + part, :]
                    cv = taps[n][0] * x if cv is None else cv + taps[n][0] * x
                    cg = taps[n][1] * x if cg is None else cg + taps[n][1] * x
                centre = (row + 1) * step + PAD + off
                half = 0.5 * cg
                value = x32[centre : centre + part, :] + cv * (half + half * jnp.tanh(half))
                o_ref[row * width + off : row * width + off + part, at] = value.astype(BF16)
        return 0

    lax.fori_loop(0, o_ref.shape[1] // LANES, tile_step, 0)


def solution(mesh):
    frames = mesh.shape["frame"]

    def on_device(queries, keys, values, residual, attn_gain, value_taps, gate_taps):
        _, rows, width, dim = queries.shape
        tokens = rows * width
        steps = -(-dim // WINDOW)
        flat = lambda a: a.reshape(tokens, dim)
        anywhere = pl.BlockSpec(memory_space=pl.ANY)
        state = (2 * steps, HEAD_DIM, LANES)
        sems = pltpu.SemaphoreType.DMA((steps,))
        two = pltpu.SemaphoreType.DMA((2,))
        ext = tokens + width
        pairs = dim // PAIR
        mixed = pl.pallas_call(
            functools.partial(mix_kernel, frames, rows, width, dim),
            out_shape=jax.ShapeDtypeStruct((tokens + 2 * width, dim), BF16),
            in_specs=[anywhere] * 4 + [pl.BlockSpec(memory_space=pltpu.VMEM)],
            out_specs=anywhere,
            scratch_shapes=[
                pltpu.VMEM((ext, dim), BF16),
                pltpu.VMEM((tokens, dim), BF16),
                pltpu.VMEM((tokens, dim), BF16),
                pltpu.VMEM((dim, tokens), BF16),
                pltpu.VMEM((ext, dim), BF16),
                pltpu.VMEM(state, F32),
            ]
            + [pltpu.VMEM(state, BF16)] * 7
            + [
                pltpu.VMEM((pairs, ext, WINDOW), BF16),
                pltpu.VMEM((pairs, ext, WINDOW), BF16),
                pltpu.VMEM((pairs, WINDOW), F32),
                pltpu.VMEM((2 * GROUP, ext, WINDOW), F32),
                pltpu.VMEM((2 * GROUP, ext, WINDOW), BF16),
                pltpu.VMEM((tokens + 2 * width, dim), BF16),
                pltpu.SemaphoreType.DMA((2, -(-dim // PIECE))),
                two,
                two,
                two,
            ]
            + [sems] * 8
            + [pltpu.SemaphoreType.DMA((pairs,))],
            compiler_params=pltpu.CompilerParams(collective_id=0, has_side_effects=True, vmem_limit_bytes=56 << 20),
        )(flat(queries), flat(keys), flat(values), flat(residual), attn_gain)
        out = pl.pallas_call(
            functools.partial(conv_kernel, rows, width),
            out_shape=jax.ShapeDtypeStruct((tokens, dim), BF16),
            grid=(-(-dim // BLOCK),),
            in_specs=[
                pl.BlockSpec((tokens + 2 * width, BLOCK), lambda c: (0, c)),
                pl.BlockSpec((9, BLOCK), lambda c: (0, c)),
                pl.BlockSpec((9, BLOCK), lambda c: (0, c)),
            ],
            out_specs=pl.BlockSpec((tokens, BLOCK), lambda c: (0, c)),
            scratch_shapes=[pltpu.VMEM(((rows + 2) * (width + 2 * PAD), LANES), F32)],
        )(mixed, value_taps, gate_taps)
        return out.reshape(1, rows, width, dim)

    placed = P(("groups", "frame"), "space", None, None)
    return jax.shard_map(
        on_device,
        mesh=mesh,
        in_specs=(placed,) * 4 + (P(),) * 3,
        out_specs=placed,
        check_vma=False,
    )
```

```python
import functools

import jax
import jax.numpy as jnp
from jax import lax
from jax.experimental import pallas as pl
from jax.experimental.pallas import tpu as pltpu
from jax.sharding import PartitionSpec as P

HEAD_DIM = 112
LANES = 128
WINDOW = 256
PAD = 8
PIECE = 384
PAIR = 2 * HEAD_DIM
LAG = 3
LEAD = 2
GROUP = 2
AHEAD = 2
F32, BF16 = jnp.float32, jnp.bfloat16


def windows(dim):
    out = []
    for lo in range(0, dim, WINDOW):
        w = min(WINDOW, dim - lo)
        h0, h1 = lo // HEAD_DIM, (lo + w - 1) // HEAD_DIM
        out.append((lo, w, range(h0, h1 + 1)))
    return out


def mix_kernel(
    frames, rows, width, dim,
    q_hbm, k_hbm, v_hbm, r_hbm, gain_hbm, vt_hbm, gt_hbm, o_ref,
    q, k, v, kt, res, st, pb, rb, ob, yb, pr, ps, vb, qa, ra, gain_ref, ga, vt_ref, gt_ref, taps, numer, sq, mixed, x32,
    kv_sem, load_sem, edge_s, edge_r, rs_s, rs_r, y_s, y_r, z_s, z_r, pv_s, pv_r, small_sem,
):
    tokens = rows * width
    tiles = st.shape[0]
    space = lax.axis_index("space")
    frame = lax.axis_index("frame")
    other = 1 - space
    pair, odd = frame // 2, frame % 2
    twin = frame + 1 - 2 * odd
    has_prev = pair > 0
    has_next = pair < frames // 2 - 1
    wins = windows(dim)
    steps = len(wins)

    cuts = list(range(0, dim, PIECE)) + [dim]
    kv_loads = []
    for i, (lo, hi) in enumerate(zip(cuts, cuts[1:])):
        kv_loads.append(
            [
                pltpu.make_async_copy(src.at[:, lo:hi], dst.at[:, lo:hi], kv_sem.at[c, i])
                for c, (src, dst) in enumerate(((k_hbm, k), (v_hbm, v)))
            ]
        )
    loads = [
        [
            pltpu.make_async_copy(src.at[:, lo:hi], dst.at[0:tokens, lo:hi], load_sem.at[c, i])
            for c, (src, dst) in enumerate(((q_hbm, q), (r_hbm, res)))
        ]
        for i, (lo, hi) in enumerate(zip(cuts, cuts[1:]))
    ]
    for copies in kv_loads:
        for copy in copies:
            copy.start()

    small = [
        pltpu.make_async_copy(src, dst, small_sem.at[i])
        for i, (src, dst) in enumerate(((gain_hbm, gain_ref), (vt_hbm, vt_ref), (gt_hbm, gt_ref)))
    ]
    for copy in small:
        copy.start()

    barrier = pltpu.get_barrier_semaphore()
    pl.semaphore_signal(barrier, inc=1, device_id={"space": other})
    pl.semaphore_signal(barrier, inc=1, device_id={"frame": twin})

    @pl.when(has_prev)
    def _():
        pl.semaphore_signal(barrier, inc=1, device_id={"frame": frame - 2})

    @pl.when(has_next)
    def _():
        pl.semaphore_signal(barrier, inc=1, device_id={"frame": frame + 2})

    st[tiles - 1] = jnp.zeros(st.shape[1:], F32)
    x32[...] = jnp.zeros(x32.shape, F32)
    taps[...] = jnp.zeros(taps.shape, F32)
    mixed[:, dim:] = jnp.zeros((mixed.shape[0], mixed.shape[1] - dim), BF16)

    def to_other(src, dst, tile, send, recv, j):
        return pltpu.make_async_remote_copy(
            src_ref=src.at[tile], dst_ref=dst.at[tile], send_sem=send.at[j], recv_sem=recv.at[j],
            device_id={"space": other},
        )

    def to_frame(src, dst, tile, send, recv, j, target):
        return pltpu.make_async_remote_copy(
            src_ref=src.at[tile], dst_ref=dst.at[tile], send_sem=send.at[j], recv_sem=recv.at[j],
            device_id={"frame": target},
        )

    edges = [
        [
            pltpu.make_async_remote_copy(
                src_ref=src.at[pl.ds(pl.multiple_of(other * (tokens - width), width), width), lo:hi],
                dst_ref=dst.at[tokens : tokens + width, lo:hi],
                send_sem=edge_s.at[c, i], recv_sem=edge_r.at[c, i], device_id={"space": other},
            )
            for c, (src, dst) in enumerate(((q_hbm, q), (r_hbm, res)))
        ]
        for i, (lo, hi) in enumerate(zip(cuts, cuts[1:]))
    ]

    def head_of(lo, w):
        return (lax.broadcasted_iota(jnp.int32, (HEAD_DIM, w), 1) + lo) // HEAD_DIM

    def own_step(j):
        tile = 2 * j + space
        to_other(pb, rb, tile, rs_s, rs_r, j).wait_recv()
        total = st[tile] + rb[tile].astype(F32)
        st[tile] = total
        ob[tile] = total.astype(BF16)
        to_frame(ob, yb, tile, y_s, y_r, j, twin).start()

    ready, turned, fetched = 0, 0, 0
    for m in range(steps):
        lo, w, heads = wins[m]
        k0, k1 = HEAD_DIM * heads[0], HEAD_DIM * (heads[-1] + 1)
        while cuts[ready] < max(k1, lo + w):
            for copy in kv_loads[ready]:
                copy.wait()
            ready += 1
        while turned < k1:
            top = min(dim, turned + LANES)
            kt[turned:top, :] = jnp.maximum(k[:, turned:top], 0).T
            turned = top
        full = jnp.dot(kt[k0:k1, :], v[:, lo : lo + w], preferred_element_type=F32)
        owner = head_of(lo, w)
        slab = full[:HEAD_DIM]
        for h in heads[1:]:
            at = HEAD_DIM * h - k0
            slab = jnp.where(owner == h, full[at : at + HEAD_DIM, :], slab)
        for part in range(-(-w // LANES)):
            tile = lo // LANES + part
            wide = min(LANES, w - part * LANES)
            st[tile, :, :wide] = slab[:, part * LANES : part * LANES + wide]
            pb[tile] = st[tile].astype(BF16)
        if m == LEAD - 1:
            pl.semaphore_wait(barrier, 2 + jnp.where(has_prev, 1, 0) + jnp.where(has_next, 1, 0))
        for n in range(m + 1) if m == LEAD - 1 else range(m, m + 1) if m >= LEAD else ():
            to_other(pb, rb, 2 * n + other, rs_s, rs_r, n).start()
        if m >= LAG:
            own_step(m - LAG)
        if m >= LEAD:
            for copies in loads[fetched : fetched + 1] + edges[fetched : fetched + 1]:
                for copy in copies:
                    copy.start()
            fetched += 1
    for copies in loads[fetched:] + edges[fetched:]:
        for copy in copies:
            copy.start()
    for m in range(max(0, steps - LAG), steps):
        own_step(m)

    def scan_step(j):
        tile = 2 * j + space
        to_frame(ob, yb, tile, y_s, y_r, j, twin).wait_recv()
        beside = yb[tile].astype(F32)

        @pl.when(has_prev)
        def _():
            to_frame(ps, pr, tile, z_s, z_r, j, frame - 2).wait_recv()

        @pl.when(jnp.logical_not(has_prev))
        def _():
            pr[tile] = jnp.zeros(pr.shape[1:], BF16)

        before = pr[tile].astype(F32)

        @pl.when(has_next)
        def _():
            ps[tile] = (before + (st[tile] + beside)).astype(BF16)
            to_frame(ps, pr, tile, z_s, z_r, j, frame + 2).start()

        vb[tile] = (before + beside * odd.astype(F32) + st[tile]).astype(BF16)
        to_other(vb, vb, tile, pv_s, pv_r, j).start()

    pairs = dim // PAIR

    def realign(r0, r1, j0, j1):
        for j in range(j0, min(j1, pairs)):
            qa[j, r0:r1, :PAIR] = jnp.maximum(q[r0:r1, PAIR * j : PAIR * (j + 1)], 0)
            ra[j, r0:r1, :PAIR] = res[r0:r1, PAIR * j : PAIR * (j + 1)]

    def cover(lo, hi, size):
        out = []
        while lo < hi:
            n = lo // size
            top = min(hi, size * (n + 1))
            out.append((n, lo - size * n, top - size * n))
            lo = top
        return out

    row_head = lax.broadcasted_iota(jnp.int32, (PAIR, PAIR), 0) < HEAD_DIM
    col_head = lax.broadcasted_iota(jnp.int32, (PAIR, PAIR), 1) < HEAD_DIM
    same = jnp.where(row_head == col_head, 1.0, 0.0).astype(BF16)
    first_head = lax.broadcasted_iota(jnp.int32, (HEAD_DIM, PAIR), 1) < HEAD_DIM

    def numer_step(j):
        parts = [vb[t, :, a:b] for t, a, b in cover(PAIR * j, PAIR * (j + 1), LANES)]
        slab = jnp.concatenate(parts, axis=1)
        zero = jnp.zeros_like(slab)
        both = jnp.concatenate([jnp.where(first_head, slab, zero), jnp.where(first_head, zero, slab)], axis=0)
        found = jnp.dot(qa[j, :, :PAIR], both, preferred_element_type=F32)
        numer[j % (2 * GROUP), :, :PAIR] = found
        sq[j % (2 * GROUP), :, :PAIR] = (found * found).astype(BF16)

    def mixed_step(j):
        total = jnp.dot(sq[j % (2 * GROUP), :, :PAIR], same, preferred_element_type=F32)
        scale = lax.rsqrt(total * (1.0 / HEAD_DIM) + 1e-6)
        normed = numer[j % (2 * GROUP), :, :PAIR] * scale
        qa[j, :, :PAIR] = (ra[j, :, :PAIR].astype(F32) + normed * ga[j : j + 1, :PAIR]).astype(BF16)
        for t in range(PAIR * j // LANES, done(j + 1)):
            lo, hi = LANES * t, min(dim, LANES * (t + 1))
            parts = [qa[n, :, a:b] for n, a, b in cover(lo, hi, PAIR)]
            mixed[:, lo:hi] = jnp.concatenate(parts, axis=1) if len(parts) > 1 else parts[0]

    def done(j):
        return -(-dim // LANES) if j == pairs else PAIR * j // LANES

    pitch = width + 2 * PAD
    far = pl.multiple_of((1 - space) * (rows + 1) * pitch + PAD, PAD)
    chunk = 16

    def conv_tile(at, keep):
        for row in range(rows):
            first = (row + 1) * pitch + PAD
            x32[first : first + width, :] = mixed[row * width : (row + 1) * width, at].astype(F32)
        x32[pl.ds(far, width), :] = mixed[tokens:, at].astype(F32)
        tv = [jnp.broadcast_to(taps[0, n : n + 1, at], (chunk, LANES)) for n in range(9)]
        tg = [jnp.broadcast_to(taps[1, n : n + 1, at], (chunk, LANES)) for n in range(9)]
        for row in range(rows):
            for off in range(0, width, chunk):
                cv, cg = None, None
                for n in range(9):
                    start = (row + n // 3) * pitch + PAD - 1 + n % 3 + off
                    x = x32[start : start + chunk, :]
                    cv = tv[n] * x if cv is None else cv + tv[n] * x
                    cg = tg[n] * x if cg is None else cg + tg[n] * x
                centre = (row + 1) * pitch + PAD + off
                half = 0.5 * cg
                value = (x32[centre : centre + chunk, :] + cv * (half + half * jnp.tanh(half))).astype(BF16)
                first = row * width + off
                if keep == LANES:
                    o_ref[first : first + chunk, at] = value
                else:
                    o_ref[first : first + chunk, dim - keep : dim] = value[:, :keep]

    def conv_step(t0, t1):
        whole = min(t1, dim // LANES)

        def one(t, _):
            conv_tile(pl.ds(pl.multiple_of(t * LANES, LANES), LANES), LANES)
            return 0

        if whole > t0:
            lax.fori_loop(t0, whole, one, 0)
        if t1 > whole:
            conv_tile(slice(whole * LANES, t1 * LANES), dim - whole * LANES)

    for copy in small:
        copy.wait()
    taps[0, 0:9, 0:dim] = vt_ref[...]
    taps[1, 0:9, 0:dim] = gt_ref[...]
    for j in range(pairs):
        ga[j : j + 1, :PAIR] = gain_ref[PAIR * j : PAIR * (j + 1)].reshape(1, PAIR)

    def prepare(stage):
        if stage == 0:
            for copies in loads:
                for copy in copies:
                    copy.wait()
        if stage == stages - 1:
            for copies in edges:
                for copy in copies:
                    copy.wait_recv()
            realign(tokens, tokens + width, 0, pairs)
        realign(0, tokens, 3 * stage, 3 * stage + 3)

    stages = -(-pairs // 3)

    @pl.when(has_prev)
    def _():
        for stage in range(stages):
            prepare(stage)

    begun = 0
    for j in range(steps + AHEAD):
        if j < steps:
            scan_step(j)
        if j < stages:
            @pl.when(jnp.logical_not(has_prev))
            def _():
                prepare(j)
        m = j - AHEAD
        if m < 0:
            continue
        to_other(vb, vb, 2 * m + other, pv_s, pv_r, m).wait_recv()
        while begun < pairs:
            until = min(pairs, begun + GROUP)
            if (PAIR * until - 1) // WINDOW > m:
                break
            for n in range(begun, until):
                numer_step(n)
            for n in range(max(0, begun - GROUP), begun):
                mixed_step(n)
            if begun:
                conv_step(done(max(0, begun - GROUP)), done(begun))
            begun = until
    last = (pairs - 1) // GROUP * GROUP
    for n in range(last, pairs):
        mixed_step(n)
    conv_step(done(last), done(pairs))

    for copies in edges:
        for copy in copies:
            copy.wait_send()

    def drain_step(j, _):
        mine, theirs = 2 * j + space, 2 * j + other
        to_other(pb, rb, theirs, rs_s, rs_r, j).wait_send()
        to_frame(ob, yb, mine, y_s, y_r, j, twin).wait_send()
        to_other(vb, vb, mine, pv_s, pv_r, j).wait_send()

        @pl.when(has_next)
        def _():
            to_frame(ps, pr, mine, z_s, z_r, j, frame + 2).wait_send()

        return 0

    lax.fori_loop(0, steps, drain_step, 0)


def solution(mesh):
    frames = mesh.shape["frame"]

    def on_device(queries, keys, values, residual, attn_gain, value_taps, gate_taps):
        _, rows, width, dim = queries.shape
        tokens = rows * width
        steps = -(-dim // WINDOW)
        flat = lambda a: a.reshape(tokens, dim)
        anywhere = pl.BlockSpec(memory_space=pl.ANY)
        state = (2 * steps, HEAD_DIM, LANES)
        sems = pltpu.SemaphoreType.DMA((steps,))
        pieces = pltpu.SemaphoreType.DMA((2, -(-dim // PIECE)))
        ext = tokens + width
        pairs = dim // PAIR
        across = -(-dim // LANES) * LANES
        operands = (flat(queries), flat(keys), flat(values), flat(residual), attn_gain, value_taps, gate_taps)
        out = pl.pallas_call(
            functools.partial(mix_kernel, frames, rows, width, dim),
            out_shape=jax.ShapeDtypeStruct((tokens, dim), BF16),
            in_specs=[anywhere] * 7,
            out_specs=pl.BlockSpec(memory_space=pltpu.VMEM),
            scratch_shapes=[
                pltpu.VMEM((ext, dim), BF16),
                pltpu.VMEM((tokens, dim), BF16),
                pltpu.VMEM((tokens, dim), BF16),
                pltpu.VMEM((dim, tokens), BF16),
                pltpu.VMEM((ext, dim), BF16),
                pltpu.VMEM(state, F32),
            ]
            + [pltpu.VMEM(state, BF16)] * 7
            + [
                pltpu.VMEM((pairs, ext, WINDOW), BF16),
                pltpu.VMEM((pairs, ext, WINDOW), BF16),
                pltpu.VMEM((dim,), F32),
                pltpu.VMEM((pairs, WINDOW), F32),
                pltpu.VMEM((9, dim), F32),
                pltpu.VMEM((9, dim), F32),
                pltpu.VMEM((2, 16, across), F32),
                pltpu.VMEM((2 * GROUP, ext, WINDOW), F32),
                pltpu.VMEM((2 * GROUP, ext, WINDOW), BF16),
                pltpu.VMEM((ext, across), BF16),
                pltpu.VMEM(((rows + 2) * (width + 2 * PAD), LANES), F32),
                pieces,
                pieces,
                pieces,
                pieces,
            ]
            + [sems] * 8
            + [pltpu.SemaphoreType.DMA((3,))],
            compiler_params=pltpu.CompilerParams(collective_id=0, has_side_effects=True, vmem_limit_bytes=50 << 20),
        )(*(pltpu.with_memory_space_constraint(a, pltpu.HBM) for a in operands))
        return out.reshape(1, rows, width, dim)

    placed = P(("groups", "frame"), "space", None, None)
    return jax.shard_map(
        on_device,
        mesh=mesh,
        in_specs=(placed,) * 4 + (P(),) * 3,
        out_specs=placed,
        check_vma=False,
    )
```

```python
import functools

import jax
import jax.numpy as jnp
from jax import lax
from jax.experimental import pallas as pl
from jax.experimental.pallas import tpu as pltpu
from jax.sharding import PartitionSpec as P

HEAD_DIM = 112
LANES = 128
WINDOW = 256
PAD = 8
PIECE = 384
PAIR = 2 * HEAD_DIM
LAG = 2
LEAD = 1
EARLY = 7
SHARE = 4
GROUP = 2
FIRST, MIDDLE, LAST = 6, 4, 2
F32, BF16 = jnp.float32, jnp.bfloat16


def windows(dim):
    out = []
    for lo in range(0, dim, WINDOW):
        w = min(WINDOW, dim - lo)
        h0, h1 = lo // HEAD_DIM, (lo + w - 1) // HEAD_DIM
        out.append((lo, w, range(h0, h1 + 1)))
    return out


def mix_kernel(
    frames, rows, width, dim,
    q_hbm, k_hbm, v_hbm, r_hbm, gain_hbm, vt_hbm, gt_hbm, o_ref,
    q, k, v, kt, res, st, pb, rb, ob, yb, pr, ps, vb, qa, ra, gain_ref, ga, vt_ref, gt_ref, taps, numer, sq, mixed, x32,
    kv_sem, load_sem, edge_s, edge_r, rs_s, rs_r, y_s, y_r, z_s, z_r, pv_s, pv_r, small_sem,
):
    tokens = rows * width
    tiles = st.shape[0]
    space = lax.axis_index("space")
    frame = lax.axis_index("frame")
    other = 1 - space
    pair, odd = frame // 2, frame % 2
    twin = frame + 1 - 2 * odd
    has_prev = pair > 0
    has_next = pair < frames // 2 - 1
    wins = windows(dim)
    steps = len(wins)

    cuts = list(range(0, dim, PIECE)) + [dim]
    kv_loads = []
    for i, (lo, hi) in enumerate(zip(cuts, cuts[1:])):
        kv_loads.append(
            [
                pltpu.make_async_copy(src.at[:, lo:hi], dst.at[:, lo:hi], kv_sem.at[c, i])
                for c, (src, dst) in enumerate(((k_hbm, k), (v_hbm, v)))
            ]
        )
    loads = [
        [
            pltpu.make_async_copy(src.at[:, lo:hi], dst.at[0:tokens, lo:hi], load_sem.at[c, i])
            for c, (src, dst) in enumerate(((q_hbm, q), (r_hbm, res)))
        ]
        for i, (lo, hi) in enumerate(zip(cuts, cuts[1:]))
    ]
    for copies in kv_loads:
        for copy in copies:
            copy.start()

    small = [
        pltpu.make_async_copy(src, dst, small_sem.at[i])
        for i, (src, dst) in enumerate(((gain_hbm, gain_ref), (vt_hbm, vt_ref), (gt_hbm, gt_ref)))
    ]
    for copy in small:
        copy.start()

    barrier = pltpu.get_barrier_semaphore()
    pl.semaphore_signal(barrier, inc=1, device_id={"space": other})
    pl.semaphore_signal(barrier, inc=1, device_id={"frame": twin})

    @pl.when(has_prev)
    def _():
        pl.semaphore_signal(barrier, inc=1, device_id={"frame": frame - 2})

    @pl.when(has_next)
    def _():
        pl.semaphore_signal(barrier, inc=1, device_id={"frame": frame + 2})

    st[tiles - 1] = jnp.zeros(st.shape[1:], F32)
    x32[...] = jnp.zeros(x32.shape, F32)
    taps[...] = jnp.zeros(taps.shape, F32)
    mixed[:, dim:] = jnp.zeros((mixed.shape[0], mixed.shape[1] - dim), BF16)

    def to_other(src, dst, tile, send, recv, j):
        return pltpu.make_async_remote_copy(
            src_ref=src.at[tile], dst_ref=dst.at[tile], send_sem=send.at[j], recv_sem=recv.at[j],
            device_id={"space": other},
        )

    cut = HEAD_DIM // 32 * 16
    halves = ((0, cut), (cut, HEAD_DIM))

    def to_frame(src, dst, tile, send, recv, j, half, target):
        r0, r1 = halves[half]
        return pltpu.make_async_remote_copy(
            src_ref=src.at[tile, r0:r1], dst_ref=dst.at[tile, r0:r1], send_sem=send.at[half, j], recv_sem=recv.at[half, j],
            device_id={"frame": target},
        )

    edges = [
        [
            pltpu.make_async_remote_copy(
                src_ref=src.at[pl.ds(pl.multiple_of(other * (tokens - width), width), width), lo:hi],
                dst_ref=dst.at[tokens : tokens + width, lo:hi],
                send_sem=edge_s.at[c, i], recv_sem=edge_r.at[c, i], device_id={"space": other},
            )
            for c, (src, dst) in enumerate(((q_hbm, q), (r_hbm, res)))
        ]
        for i, (lo, hi) in enumerate(zip(cuts, cuts[1:]))
    ]

    def head_of(lo, w):
        return (lax.broadcasted_iota(jnp.int32, (HEAD_DIM, w), 1) + lo) // HEAD_DIM

    def own_step(j):
        tile = 2 * j + space
        to_other(pb, rb, tile, rs_s, rs_r, j).wait_recv()
        total = st[tile] + rb[tile].astype(F32)
        st[tile] = total
        ob[tile] = total.astype(BF16)
        for half in range(2):
            to_frame(ob, yb, tile, y_s, y_r, j, half, twin).start()

    def scan_step(j, lead):
        tile = 2 * j + space
        for half, (r0, r1) in enumerate(halves):
            to_frame(ob, yb, tile, y_s, y_r, j, half, twin).wait_recv()
            beside = yb[tile, r0:r1].astype(F32)
            mine = st[tile, r0:r1]
            if lead:
                before = jnp.zeros_like(mine)
            else:
                to_frame(ps, pr, tile, z_s, z_r, j, half, frame - 2).wait_recv()
                before = pr[tile, r0:r1].astype(F32)

            @pl.when(has_next)
            def _():
                ps[tile, r0:r1] = (before + (mine + beside)).astype(BF16)
                to_frame(ps, pr, tile, z_s, z_r, j, half, frame + 2).start()

            vb[tile, r0:r1] = (before + beside * odd.astype(F32) + mine).astype(BF16)
        to_other(vb, vb, tile, pv_s, pv_r, j).start()

    ready, turned, fetched = 0, 0, 0
    for m in range(steps):
        lo, w, heads = wins[m]
        k0, k1 = HEAD_DIM * heads[0], HEAD_DIM * (heads[-1] + 1)
        while cuts[ready] < max(k1, lo + w):
            for copy in kv_loads[ready]:
                copy.wait()
            ready += 1
        while turned < k1:
            top = min(dim, turned + LANES)
            kt[turned:top, :] = jnp.maximum(k[:, turned:top], 0).T
            turned = top
        full = jnp.dot(kt[k0:k1, :], v[:, lo : lo + w], preferred_element_type=F32)
        owner = head_of(lo, w)
        slab = full[:HEAD_DIM]
        for h in heads[1:]:
            at = HEAD_DIM * h - k0
            slab = jnp.where(owner == h, full[at : at + HEAD_DIM, :], slab)
        for part in range(-(-w // LANES)):
            tile = lo // LANES + part
            wide = min(LANES, w - part * LANES)
            st[tile, :, :wide] = slab[:, part * LANES : part * LANES + wide]
            pb[tile] = st[tile].astype(BF16)
        if m == LEAD - 1:
            pl.semaphore_wait(barrier, 2 + jnp.where(has_prev, 1, 0) + jnp.where(has_next, 1, 0))
        for n in range(m + 1) if m == LEAD - 1 else range(m, m + 1) if m >= LEAD else ():
            to_other(pb, rb, 2 * n + other, rs_s, rs_r, n).start()
        if m >= LAG:
            own_step(m - LAG)
        if m >= LEAD:
            for copies in loads[fetched : fetched + 1] + edges[fetched : fetched + 1]:
                for copy in copies:
                    copy.start()
            fetched += 1
        if m >= EARLY:
            @pl.when(jnp.logical_not(has_prev))
            def _():
                scan_step(m - EARLY, True)
    for copies in loads[fetched:] + edges[fetched:]:
        for copy in copies:
            copy.start()
    for m in range(max(0, steps - LAG), steps):
        own_step(m)

    pairs = dim // PAIR

    def realign(r0, r1, j0, j1):
        for j in range(j0, min(j1, pairs)):
            qa[j, r0:r1, :PAIR] = jnp.maximum(q[r0:r1, PAIR * j : PAIR * (j + 1)], 0)
            ra[j, r0:r1, :PAIR] = res[r0:r1, PAIR * j : PAIR * (j + 1)]

    def cover(lo, hi, size):
        out = []
        while lo < hi:
            n = lo // size
            top = min(hi, size * (n + 1))
            out.append((n, lo - size * n, top - size * n))
            lo = top
        return out

    row_head = lax.broadcasted_iota(jnp.int32, (PAIR, PAIR), 0) < HEAD_DIM
    col_head = lax.broadcasted_iota(jnp.int32, (PAIR, PAIR), 1) < HEAD_DIM
    same = jnp.where(row_head == col_head, 1.0, 0.0).astype(BF16)
    first_head = lax.broadcasted_iota(jnp.int32, (HEAD_DIM, PAIR), 1) < HEAD_DIM

    def numer_step(j):
        parts = [vb[t, :, a:b] for t, a, b in cover(PAIR * j, PAIR * (j + 1), LANES)]
        slab = jnp.concatenate(parts, axis=1)
        zero = jnp.zeros_like(slab)
        both = jnp.concatenate([jnp.where(first_head, slab, zero), jnp.where(first_head, zero, slab)], axis=0)
        found = jnp.dot(qa[j, :, :PAIR], both, preferred_element_type=F32)
        numer[j % (2 * GROUP), :, :PAIR] = found
        sq[j % (2 * GROUP), :, :PAIR] = (found * found).astype(BF16)

    def mixed_step(j):
        total = jnp.dot(sq[j % (2 * GROUP), :, :PAIR], same, preferred_element_type=F32)
        scale = lax.rsqrt(total * (1.0 / HEAD_DIM) + 1e-6)
        normed = numer[j % (2 * GROUP), :, :PAIR] * scale
        qa[j, :, :PAIR] = (ra[j, :, :PAIR].astype(F32) + normed * ga[j : j + 1, :PAIR]).astype(BF16)
        for t in range(PAIR * j // LANES, done(j + 1)):
            lo, hi = LANES * t, min(dim, LANES * (t + 1))
            parts = [qa[n, :, a:b] for n, a, b in cover(lo, hi, PAIR)]
            mixed[:, lo:hi] = jnp.concatenate(parts, axis=1) if len(parts) > 1 else parts[0]

    def done(j):
        return -(-dim // LANES) if j == pairs else PAIR * j // LANES

    pitch = width + 2 * PAD
    far = pl.multiple_of((1 - space) * (rows + 1) * pitch + PAD, PAD)
    chunk = 16

    def conv_tile(at, keep):
        for row in range(rows):
            first = (row + 1) * pitch + PAD
            x32[first : first + width, :] = mixed[row * width : (row + 1) * width, at].astype(F32)
        x32[pl.ds(far, width), :] = mixed[tokens:, at].astype(F32)
        tv = [jnp.broadcast_to(taps[0, n : n + 1, at], (chunk, LANES)) for n in range(9)]
        tg = [jnp.broadcast_to(taps[1, n : n + 1, at], (chunk, LANES)) for n in range(9)]
        for row in range(rows):
            for off in range(0, width, chunk):
                cv, cg = None, None
                for n in range(9):
                    start = (row + n // 3) * pitch + PAD - 1 + n % 3 + off
                    x = x32[start : start + chunk, :]
                    cv = tv[n] * x if cv is None else cv + tv[n] * x
                    cg = tg[n] * x if cg is None else cg + tg[n] * x
                centre = (row + 1) * pitch + PAD + off
                half = 0.5 * cg
                value = (x32[centre : centre + chunk, :] + cv * (half + half * jnp.tanh(half))).astype(BF16)
                first = row * width + off
                if keep == LANES:
                    o_ref[first : first + chunk, at] = value
                else:
                    o_ref[first : first + chunk, dim - keep : dim] = value[:, :keep]

    def conv_step(t0, t1):
        whole = min(t1, dim // LANES)

        def one(t, _):
            conv_tile(pl.ds(pl.multiple_of(t * LANES, LANES), LANES), LANES)
            return 0

        if whole > t0:
            lax.fori_loop(t0, whole, one, 0)
        if t1 > whole:
            conv_tile(slice(whole * LANES, t1 * LANES), dim - whole * LANES)

    for copy in small:
        copy.wait()
    taps[0, 0:9, 0:dim] = vt_ref[...]
    taps[1, 0:9, 0:dim] = gt_ref[...]
    for j in range(pairs):
        ga[j : j + 1, :PAIR] = gain_ref[PAIR * j : PAIR * (j + 1)].reshape(1, PAIR)

    def prepare(stage):
        if stage == 0:
            for copies in loads:
                for copy in copies:
                    copy.wait()
        if stage == stages - 1:
            for copies in edges:
                for copy in copies:
                    copy.wait_recv()
            realign(tokens, tokens + width, 0, pairs)
        realign(0, tokens, SHARE * stage, SHARE * (stage + 1))

    stages = -(-pairs // SHARE)
    deep = pair > 1

    @pl.when(deep)
    def _():
        for stage in range(stages):
            prepare(stage)

    begun = 0
    for m in range(-max(FIRST, MIDDLE, LAST, stages), steps):
        if steps - EARLY <= m + FIRST < steps:
            @pl.when(jnp.logical_not(has_prev))
            def _():
                scan_step(m + FIRST, True)

        if 0 <= m + MIDDLE < steps:
            @pl.when(jnp.logical_and(has_prev, has_next))
            def _():
                scan_step(m + MIDDLE, False)

        if 0 <= m + LAST < steps:
            @pl.when(jnp.logical_and(has_prev, jnp.logical_not(has_next)))
            def _():
                scan_step(m + LAST, False)

        if 0 <= m + stages < stages:
            @pl.when(jnp.logical_not(deep))
            def _():
                prepare(m + stages)

        if m < 0:
            continue
        to_other(vb, vb, 2 * m + other, pv_s, pv_r, m).wait_recv()
        while begun < pairs:
            until = min(pairs, begun + GROUP)
            if (PAIR * until - 1) // WINDOW > m:
                break
            for n in range(begun, until):
                numer_step(n)
            for n in range(max(0, begun - GROUP), begun):
                mixed_step(n)
            if begun:
                conv_step(done(max(0, begun - GROUP)), done(begun))
            begun = until
    last = (pairs - 1) // GROUP * GROUP
    for n in range(last, pairs):
        mixed_step(n)
    conv_step(done(last), done(pairs))

    for copies in edges:
        for copy in copies:
            copy.wait_send()

    def drain_step(j, _):
        mine, theirs = 2 * j + space, 2 * j + other
        to_other(pb, rb, theirs, rs_s, rs_r, j).wait_send()
        for half in range(2):
            to_frame(ob, yb, mine, y_s, y_r, j, half, twin).wait_send()
        to_other(vb, vb, mine, pv_s, pv_r, j).wait_send()

        @pl.when(has_next)
        def _():
            for half in range(2):
                to_frame(ps, pr, mine, z_s, z_r, j, half, frame + 2).wait_send()

        return 0

    lax.fori_loop(0, steps, drain_step, 0)


def solution(mesh):
    frames = mesh.shape["frame"]

    def on_device(queries, keys, values, residual, attn_gain, value_taps, gate_taps):
        _, rows, width, dim = queries.shape
        tokens = rows * width
        steps = -(-dim // WINDOW)
        flat = lambda a: a.reshape(tokens, dim)
        anywhere = pl.BlockSpec(memory_space=pl.ANY)
        state = (2 * steps, HEAD_DIM, LANES)
        sems = pltpu.SemaphoreType.DMA((steps,))
        pieces = pltpu.SemaphoreType.DMA((2, -(-dim // PIECE)))
        ext = tokens + width
        pairs = dim // PAIR
        across = -(-dim // LANES) * LANES
        operands = (flat(queries), flat(keys), flat(values), flat(residual), attn_gain, value_taps, gate_taps)
        out = pl.pallas_call(
            functools.partial(mix_kernel, frames, rows, width, dim),
            out_shape=jax.ShapeDtypeStruct((tokens, dim), BF16),
            in_specs=[anywhere] * 7,
            out_specs=pl.BlockSpec(memory_space=pltpu.VMEM),
            scratch_shapes=[
                pltpu.VMEM((ext, dim), BF16),
                pltpu.VMEM((tokens, dim), BF16),
                pltpu.VMEM((tokens, dim), BF16),
                pltpu.VMEM((dim, tokens), BF16),
                pltpu.VMEM((ext, dim), BF16),
                pltpu.VMEM(state, F32),
            ]
            + [pltpu.VMEM(state, BF16)] * 7
            + [
                pltpu.VMEM((pairs, ext, WINDOW), BF16),
                pltpu.VMEM((pairs, ext, WINDOW), BF16),
                pltpu.VMEM((dim,), F32),
                pltpu.VMEM((pairs, WINDOW), F32),
                pltpu.VMEM((9, dim), F32),
                pltpu.VMEM((9, dim), F32),
                pltpu.VMEM((2, 16, across), F32),
                pltpu.VMEM((2 * GROUP, ext, WINDOW), F32),
                pltpu.VMEM((2 * GROUP, ext, WINDOW), BF16),
                pltpu.VMEM((ext, across), BF16),
                pltpu.VMEM(((rows + 2) * (width + 2 * PAD), LANES), F32),
                pieces,
                pieces,
                pieces,
                pieces,
            ]
            + [sems] * 2
            + [pltpu.SemaphoreType.DMA((2, steps))] * 4
            + [sems] * 2
            + [pltpu.SemaphoreType.DMA((3,))],
            compiler_params=pltpu.CompilerParams(collective_id=0, has_side_effects=True, vmem_limit_bytes=50 << 20),
        )(*(pltpu.with_memory_space_constraint(a, pltpu.HBM) for a in operands))
        return out.reshape(1, rows, width, dim)

    placed = P(("groups", "frame"), "space", None, None)
    return jax.shard_map(
        on_device,
        mesh=mesh,
        in_specs=(placed,) * 4 + (P(),) * 3,
        out_specs=placed,
        check_vma=False,
    )
```

```python
import functools

import jax
import jax.numpy as jnp
from jax import lax
from jax.experimental import pallas as pl
from jax.experimental.pallas import tpu as pltpu
from jax.sharding import PartitionSpec as P

HEAD_DIM = 112
LANES = 128
WINDOW = 256
PAD = 8
PIECE = 384
PAIR = 2 * HEAD_DIM
LAG = 2
LEAD = 1
EARLY = 7
SHARE = 4
GROUP = 2
FIRST, MIDDLE, LAST = 6, 4, 2
F32, BF16 = jnp.float32, jnp.bfloat16


def windows(dim):
    out = []
    for lo in range(0, dim, WINDOW):
        w = min(WINDOW, dim - lo)
        h0, h1 = lo // HEAD_DIM, (lo + w - 1) // HEAD_DIM
        out.append((lo, w, range(h0, h1 + 1)))
    return out


def mix_kernel(
    frames, rows, width, dim,
    q_hbm, k_hbm, v_hbm, r_hbm, gain_hbm, vt_hbm, gt_hbm, o_ref,
    q, k, v, kt, res, st, pb, rb, ob, yb, pr, ps, vb, qa, ra, gain_ref, ga, vt_ref, gt_ref, taps, numer, sq, mixed, x32, left, right,
    kv_sem, load_sem, edge_s, edge_r, rs_s, rs_r, y_s, y_r, z_s, z_r, pv_s, pv_r, small_sem,
):
    tokens = rows * width
    tiles = st.shape[0]
    space = lax.axis_index("space")
    frame = lax.axis_index("frame")
    other = 1 - space
    pair, odd = frame // 2, frame % 2
    twin = frame + 1 - 2 * odd
    has_prev = pair > 0
    has_next = pair < frames // 2 - 1
    wins = windows(dim)
    steps = len(wins)

    cuts = list(range(0, dim, PIECE)) + [dim]
    kv_loads = []
    for i, (lo, hi) in enumerate(zip(cuts, cuts[1:])):
        kv_loads.append(
            [
                pltpu.make_async_copy(src.at[:, lo:hi], dst.at[:, lo:hi], kv_sem.at[c, i])
                for c, (src, dst) in enumerate(((k_hbm, k), (v_hbm, v)))
            ]
        )
    loads = [
        [
            pltpu.make_async_copy(src.at[:, lo:hi], dst.at[0:tokens, lo:hi], load_sem.at[c, i])
            for c, (src, dst) in enumerate(((q_hbm, q), (r_hbm, res)))
        ]
        for i, (lo, hi) in enumerate(zip(cuts, cuts[1:]))
    ]
    for copies in kv_loads:
        for copy in copies:
            copy.start()

    small = [
        pltpu.make_async_copy(src, dst, small_sem.at[i])
        for i, (src, dst) in enumerate(((gain_hbm, gain_ref), (vt_hbm, vt_ref), (gt_hbm, gt_ref)))
    ]
    for copy in small:
        copy.start()

    barrier = pltpu.get_barrier_semaphore()
    pl.semaphore_signal(barrier, inc=1, device_id={"space": other})
    pl.semaphore_signal(barrier, inc=1, device_id={"frame": twin})

    @pl.when(has_prev)
    def _():
        pl.semaphore_signal(barrier, inc=1, device_id={"frame": frame - 2})

    @pl.when(has_next)
    def _():
        pl.semaphore_signal(barrier, inc=1, device_id={"frame": frame + 2})

    st[tiles - 1] = jnp.zeros(st.shape[1:], F32)
    x32[...] = jnp.zeros(x32.shape, F32)
    taps[...] = jnp.zeros(taps.shape, F32)
    mixed[:, dim:] = jnp.zeros((mixed.shape[0], mixed.shape[1] - dim), BF16)
    mixed[pl.ds(pl.multiple_of(space * (tokens + width), width), width), :] = jnp.zeros((width, mixed.shape[1]), BF16)

    def to_other(src, dst, tile, send, recv, j):
        return pltpu.make_async_remote_copy(
            src_ref=src.at[tile], dst_ref=dst.at[tile], send_sem=send.at[0], recv_sem=recv.at[j],
            device_id={"space": other},
        )

    cut = HEAD_DIM // 32 * 16
    halves = ((0, cut), (cut, HEAD_DIM))

    def to_frame(src, dst, tile, send, recv, j, half, target):
        r0, r1 = halves[half]
        return pltpu.make_async_remote_copy(
            src_ref=src.at[tile, r0:r1], dst_ref=dst.at[tile, r0:r1], send_sem=send.at[0], recv_sem=recv.at[half, j],
            device_id={"frame": target},
        )

    edges = [
        [
            pltpu.make_async_remote_copy(
                src_ref=src.at[pl.ds(pl.multiple_of(other * (tokens - width), width), width), lo:hi],
                dst_ref=dst.at[tokens : tokens + width, lo:hi],
                send_sem=edge_s.at[c, i], recv_sem=edge_r.at[c, i], device_id={"space": other},
            )
            for c, (src, dst) in enumerate(((q_hbm, q), (r_hbm, res)))
        ]
        for i, (lo, hi) in enumerate(zip(cuts, cuts[1:]))
    ]

    def head_of(lo, w):
        return (lax.broadcasted_iota(jnp.int32, (HEAD_DIM, w), 1) + lo) // HEAD_DIM

    def own_step(j):
        tile = 2 * j + space
        to_other(pb, rb, tile, rs_s, rs_r, j).wait_recv()
        total = st[tile] + rb[tile].astype(F32)
        st[tile] = total
        ob[tile] = total.astype(BF16)
        for half in range(2):
            to_frame(ob, yb, tile, y_s, y_r, j, half, twin).start()

    def scan_step(j, lead):
        tile = 2 * j + space
        for half, (r0, r1) in enumerate(halves):
            to_frame(ob, yb, tile, y_s, y_r, j, half, twin).wait_recv()
            beside = yb[tile, r0:r1].astype(F32)
            mine = st[tile, r0:r1]
            if lead:
                before = jnp.zeros_like(mine)
            else:
                to_frame(ps, pr, tile, z_s, z_r, j, half, frame - 2).wait_recv()
                before = pr[tile, r0:r1].astype(F32)

            @pl.when(has_next)
            def _():
                ps[tile, r0:r1] = (before + (mine + beside)).astype(BF16)
                to_frame(ps, pr, tile, z_s, z_r, j, half, frame + 2).start()

            vb[tile, r0:r1] = (before + beside * odd.astype(F32) + mine).astype(BF16)
        to_other(vb, vb, tile, pv_s, pv_r, j).start()

    ready, turned, fetched = 0, 0, 0
    for m in range(steps):
        lo, w, heads = wins[m]
        k0, k1 = HEAD_DIM * heads[0], HEAD_DIM * (heads[-1] + 1)
        while cuts[ready] < max(k1, lo + w):
            for copy in kv_loads[ready]:
                copy.wait()
            ready += 1
        while turned < k1:
            top = min(dim, turned + LANES)
            kt[turned:top, :] = jnp.maximum(k[:, turned:top], 0).T
            turned = top
        full = jnp.dot(kt[k0:k1, :], v[:, lo : lo + w], preferred_element_type=F32)
        owner = head_of(lo, w)
        slab = full[:HEAD_DIM]
        for h in heads[1:]:
            at = HEAD_DIM * h - k0
            slab = jnp.where(owner == h, full[at : at + HEAD_DIM, :], slab)
        for part in range(-(-w // LANES)):
            tile = lo // LANES + part
            wide = min(LANES, w - part * LANES)
            st[tile, :, :wide] = slab[:, part * LANES : part * LANES + wide]
            pb[tile] = st[tile].astype(BF16)
        if m == LEAD - 1:
            pl.semaphore_wait(barrier, 2 + jnp.where(has_prev, 1, 0) + jnp.where(has_next, 1, 0))
        for n in range(m + 1) if m == LEAD - 1 else range(m, m + 1) if m >= LEAD else ():
            to_other(pb, rb, 2 * n + other, rs_s, rs_r, n).start()
        if m >= LAG:
            own_step(m - LAG)
        if m >= LEAD:
            for copies in loads[fetched : fetched + 1] + edges[fetched : fetched + 1]:
                for copy in copies:
                    copy.start()
            fetched += 1
        if m >= EARLY:
            @pl.when(jnp.logical_not(has_prev))
            def _():
                scan_step(m - EARLY, True)
    for copies in loads[fetched:] + edges[fetched:]:
        for copy in copies:
            copy.start()
    for m in range(max(0, steps - LAG), steps):
        own_step(m)

    pairs = dim // PAIR

    def realign(r0, r1, j0, j1):
        for j in range(j0, min(j1, pairs)):
            qa[j, r0:r1, :PAIR] = jnp.maximum(q[r0:r1, PAIR * j : PAIR * (j + 1)], 0)
            ra[j, r0:r1, :PAIR] = res[r0:r1, PAIR * j : PAIR * (j + 1)]

    def cover(lo, hi, size):
        out = []
        while lo < hi:
            n = lo // size
            top = min(hi, size * (n + 1))
            out.append((n, lo - size * n, top - size * n))
            lo = top
        return out

    row_head = lax.broadcasted_iota(jnp.int32, (PAIR, PAIR), 0) < HEAD_DIM
    col_head = lax.broadcasted_iota(jnp.int32, (PAIR, PAIR), 1) < HEAD_DIM
    same = jnp.where(row_head == col_head, 1.0, 0.0).astype(BF16)
    first_head = lax.broadcasted_iota(jnp.int32, (HEAD_DIM, PAIR), 1) < HEAD_DIM

    def numer_step(j):
        parts = [vb[t, :, a:b] for t, a, b in cover(PAIR * j, PAIR * (j + 1), LANES)]
        slab = jnp.concatenate(parts, axis=1)
        zero = jnp.zeros_like(slab)
        both = jnp.concatenate([jnp.where(first_head, slab, zero), jnp.where(first_head, zero, slab)], axis=0)
        found = jnp.dot(qa[j, :, :PAIR], both, preferred_element_type=F32)
        numer[j % (2 * GROUP), :, :PAIR] = found
        sq[j % (2 * GROUP), :, :PAIR] = (found * found).astype(BF16)

    def mixed_step(j):
        total = jnp.dot(sq[j % (2 * GROUP), :, :PAIR], same, preferred_element_type=F32)
        scale = lax.rsqrt(total * (1.0 / HEAD_DIM) + 1e-6)
        normed = numer[j % (2 * GROUP), :, :PAIR] * scale
        qa[j, :, :PAIR] = (ra[j, :, :PAIR].astype(F32) + normed * ga[j : j + 1, :PAIR]).astype(BF16)
        for t in range(PAIR * j // LANES, done(j + 1)):
            lo, hi = LANES * t, min(dim, LANES * (t + 1))
            parts = [qa[n, :, a:b] for n, a, b in cover(lo, hi, PAIR)]
            value = jnp.concatenate(parts, axis=1) if len(parts) > 1 else parts[0]
            mixed[width : width + tokens, lo:hi] = value[:tokens]
            mixed[far, lo:hi] = value[tokens:]

    def done(j):
        return -(-dim // LANES) if j == pairs else PAIR * j // LANES

    pitch = width + 2 * PAD
    far = pl.ds(pl.multiple_of((1 - space) * (tokens + width), width), width)
    chunk = 16

    def tree(terms):
        total = terms[0]
        for term in terms[1:]:
            total = total + term
        return total

    def conv_tile(at, keep):
        for row in range(rows + 2):
            first = row * pitch + PAD
            x32[first : first + width, :] = mixed[row * width : (row + 1) * width, at].astype(F32)
        for row in range(rows + 2):
            first = row * pitch + PAD
            here = slice(row * width, (row + 1) * width)
            left[here, :] = x32[first - 1 : first - 1 + width, :].astype(BF16)
            right[here, :] = x32[first + 1 : first + 1 + width, :].astype(BF16)
        tv, tg = ([jnp.broadcast_to(taps[f, n : n + 1, at], (chunk, LANES)).astype(BF16) for n in range(9)] for f in range(2))
        for row in range(rows):
            for off in range(0, width, chunk):
                cv = half = None
                for n in range(9):
                    start = (row + n // 3) * width + off
                    here = slice(start, start + chunk)
                    x = left[here, :] if n % 3 == 0 else mixed[here, at] if n % 3 == 1 else right[here, :]
                    cv = tv[n] * x if cv is None else cv + tv[n] * x
                    half = tg[n] * x if half is None else half + tg[n] * x
                cv, half = cv.astype(F32), half.astype(F32)
                centre = (row + 1) * pitch + PAD + off
                value = (x32[centre : centre + chunk, :] + cv * (half + half * jnp.tanh(half))).astype(BF16)
                first = row * width + off
                if keep == LANES:
                    o_ref[first : first + chunk, at] = value
                else:
                    o_ref[first : first + chunk, dim - keep : dim] = value[:, :keep]

    def conv_step(t0, t1):
        whole = min(t1, dim // LANES)

        def one(t, _):
            conv_tile(pl.ds(pl.multiple_of(t * LANES, LANES), LANES), LANES)
            return 0

        if whole > t0:
            lax.fori_loop(t0, whole, one, 0)
        if t1 > whole:
            conv_tile(slice(whole * LANES, t1 * LANES), dim - whole * LANES)

    for copy in small:
        copy.wait()
    taps[0, 0:9, 0:dim] = vt_ref[...]
    taps[1, 0:9, 0:dim] = 0.5 * gt_ref[...]
    for j in range(pairs):
        ga[j : j + 1, :PAIR] = gain_ref[PAIR * j : PAIR * (j + 1)].reshape(1, PAIR)

    def prepare(stage):
        if stage == 0:
            for copies in loads:
                for copy in copies:
                    copy.wait()
        if stage == stages - 1:
            for copies in edges:
                for copy in copies:
                    copy.wait_recv()
            realign(tokens, tokens + width, 0, pairs)
        realign(0, tokens, SHARE * stage, SHARE * (stage + 1))

    stages = -(-pairs // SHARE)
    deep = pair > 1

    @pl.when(deep)
    def _():
        for stage in range(stages):
            prepare(stage)

    begun = 0
    for m in range(-max(FIRST, MIDDLE, LAST, stages), steps):
        if steps - EARLY <= m + FIRST < steps:
            @pl.when(jnp.logical_not(has_prev))
            def _():
                scan_step(m + FIRST, True)

        if 0 <= m + MIDDLE < steps:
            @pl.when(jnp.logical_and(has_prev, has_next))
            def _():
                scan_step(m + MIDDLE, False)

        if 0 <= m + LAST < steps:
            @pl.when(jnp.logical_and(has_prev, jnp.logical_not(has_next)))
            def _():
                scan_step(m + LAST, False)

        if 0 <= m + stages < stages:
            @pl.when(jnp.logical_not(deep))
            def _():
                prepare(m + stages)

        if m < 0:
            continue
        to_other(vb, vb, 2 * m + other, pv_s, pv_r, m).wait_recv()
        while begun < pairs:
            until = min(pairs, begun + GROUP)
            if (PAIR * until - 1) // WINDOW > m:
                break
            for n in range(begun, until):
                numer_step(n)
            for n in range(max(0, begun - GROUP), begun):
                mixed_step(n)
            if begun:
                conv_step(done(max(0, begun - GROUP)), done(begun))
            begun = until
    last = (pairs - 1) // GROUP * GROUP
    for n in range(last, pairs):
        mixed_step(n)
    conv_step(done(last), done(pairs))

    for copies in edges:
        for copy in copies:
            copy.wait_send()

    def drain(buf, send, recv, target):
        pltpu.make_async_remote_copy(
            src_ref=buf.at[0:steps], dst_ref=buf.at[0:steps], send_sem=send.at[0], recv_sem=recv, device_id=target
        ).wait_send()

    drain(pb, rs_s, rs_r.at[0], {"space": other})
    drain(ob, y_s, y_r.at[0, 0], {"frame": twin})
    drain(vb, pv_s, pv_r.at[0], {"space": other})

    @pl.when(has_next)
    def _():
        drain(ps, z_s, z_r.at[0, 0], {"frame": frame + 2})


def solution(mesh):
    frames = mesh.shape["frame"]

    def on_device(queries, keys, values, residual, attn_gain, value_taps, gate_taps):
        _, rows, width, dim = queries.shape
        tokens = rows * width
        steps = -(-dim // WINDOW)
        flat = lambda a: a.reshape(tokens, dim)
        anywhere = pl.BlockSpec(memory_space=pl.ANY)
        state = (2 * steps, HEAD_DIM, LANES)
        one, sems, split = (pltpu.SemaphoreType.DMA(n) for n in ((1,), (steps,), (2, steps)))
        pieces = pltpu.SemaphoreType.DMA((2, -(-dim // PIECE)))
        ext = tokens + width
        pairs = dim // PAIR
        across = -(-dim // LANES) * LANES
        operands = (flat(queries), flat(keys), flat(values), flat(residual), attn_gain, value_taps, gate_taps)
        out = pl.pallas_call(
            functools.partial(mix_kernel, frames, rows, width, dim),
            out_shape=jax.ShapeDtypeStruct((tokens, dim), BF16),
            in_specs=[anywhere] * 7,
            out_specs=pl.BlockSpec(memory_space=pltpu.VMEM),
            scratch_shapes=[
                pltpu.VMEM((ext, dim), BF16),
                pltpu.VMEM((tokens, dim), BF16),
                pltpu.VMEM((tokens, dim), BF16),
                pltpu.VMEM((dim, tokens), BF16),
                pltpu.VMEM((ext, dim), BF16),
                pltpu.VMEM(state, F32),
            ]
            + [pltpu.VMEM(state, BF16)] * 7
            + [
                pltpu.VMEM((pairs, ext, WINDOW), BF16),
                pltpu.VMEM((pairs, ext, WINDOW), BF16),
                pltpu.VMEM((dim,), F32),
                pltpu.VMEM((pairs, WINDOW), F32),
                pltpu.VMEM((9, dim), F32),
                pltpu.VMEM((9, dim), F32),
                pltpu.VMEM((2, 16, across), F32),
                pltpu.VMEM((2 * GROUP, ext, WINDOW), F32),
                pltpu.VMEM((2 * GROUP, ext, WINDOW), BF16),
                pltpu.VMEM((ext + width, across), BF16),
                pltpu.VMEM(((rows + 2) * (width + 2 * PAD), LANES), F32),
                pltpu.VMEM((ext + width, LANES), BF16),
                pltpu.VMEM((ext + width, LANES), BF16),
                pieces,
                pieces,
                pieces,
                pieces,
            ]
            + [one, sems, one, split, one, split, one, sems]
            + [pltpu.SemaphoreType.DMA((3,))],
            compiler_params=pltpu.CompilerParams(collective_id=0, has_side_effects=True, vmem_limit_bytes=50 << 20),
        )(*(pltpu.with_memory_space_constraint(a, pltpu.HBM) for a in operands))
        return out.reshape(1, rows, width, dim)

    placed = P(("groups", "frame"), "space", None, None)
    return jax.shard_map(
        on_device,
        mesh=mesh,
        in_specs=(placed,) * 4 + (P(),) * 3,
        out_specs=placed,
        check_vma=False,
    )
```

```python
import functools

import jax
import jax.numpy as jnp
from jax import lax
from jax.experimental import pallas as pl
from jax.experimental.pallas import tpu as pltpu
from jax.sharding import PartitionSpec as P

HEAD_DIM = 112
LANES = 128
WINDOW = 256
PAD = 8
PIECE = 384
PAIR = 2 * HEAD_DIM
LAG = 2
LEAD = 1
EARLY = 7
SHARE = 4
GROUP = 2
SINGLES = 4
FIRST, MIDDLE, LAST = 6, 4, 2
F32, BF16 = jnp.float32, jnp.bfloat16


def windows(dim):
    out = []
    for lo in range(0, dim, WINDOW):
        w = min(WINDOW, dim - lo)
        h0, h1 = lo // HEAD_DIM, (lo + w - 1) // HEAD_DIM
        out.append((lo, w, range(h0, h1 + 1)))
    return out


def mix_kernel(
    frames, rows, width, dim,
    q_hbm, k_hbm, v_hbm, r_hbm, gain_hbm, vt_hbm, gt_hbm, o_ref,
    q, k, v, kt, res, st, pb, rb, ob, yb, pr, ps, vb, qa, ra, gain_ref, ga, vt_ref, gt_ref, taps, numer, sq, mixed, x32, left, right,
    kv_sem, load_sem, edge_s, edge_r, rs_s, rs_r, y_s, y_r, z_s, z_r, pv_s, pv_r, small_sem,
):
    tokens = rows * width
    tiles = st.shape[0]
    space = lax.axis_index("space")
    frame = lax.axis_index("frame")
    other = 1 - space
    pair, odd = frame // 2, frame % 2
    twin = frame + 1 - 2 * odd
    has_prev = pair > 0
    has_next = pair < frames // 2 - 1
    wins = windows(dim)
    steps = len(wins)

    cuts = list(range(0, dim, PIECE)) + [dim]
    kv_loads = []
    for i, (lo, hi) in enumerate(zip(cuts, cuts[1:])):
        kv_loads.append(
            [
                pltpu.make_async_copy(src.at[:, lo:hi], dst.at[:, lo:hi], kv_sem.at[c, i])
                for c, (src, dst) in enumerate(((k_hbm, k), (v_hbm, v)))
            ]
        )
    loads = [
        [
            pltpu.make_async_copy(src.at[:, lo:hi], dst.at[0:tokens, lo:hi], load_sem.at[c, i])
            for c, (src, dst) in enumerate(((q_hbm, q), (r_hbm, res)))
        ]
        for i, (lo, hi) in enumerate(zip(cuts, cuts[1:]))
    ]
    for copies in kv_loads:
        for copy in copies:
            copy.start()

    small = [
        pltpu.make_async_copy(src, dst, small_sem.at[i])
        for i, (src, dst) in enumerate(((gain_hbm, gain_ref), (vt_hbm, vt_ref), (gt_hbm, gt_ref)))
    ]
    for copy in small:
        copy.start()

    barrier = pltpu.get_barrier_semaphore()
    pl.semaphore_signal(barrier, inc=1, device_id={"space": other})
    pl.semaphore_signal(barrier, inc=1, device_id={"frame": twin})

    @pl.when(has_prev)
    def _():
        pl.semaphore_signal(barrier, inc=1, device_id={"frame": frame - 2})

    @pl.when(has_next)
    def _():
        pl.semaphore_signal(barrier, inc=1, device_id={"frame": frame + 2})

    st[tiles - 1] = jnp.zeros(st.shape[1:], F32)
    x32[...] = jnp.zeros(x32.shape, F32)
    taps[...] = jnp.zeros(taps.shape, F32)
    mixed[:, dim:] = jnp.zeros((mixed.shape[0], mixed.shape[1] - dim), BF16)
    mixed[pl.ds(pl.multiple_of(space * (tokens + width), width), width), :] = jnp.zeros((width, mixed.shape[1]), BF16)

    def to_other(src, dst, tile, send, recv, j):
        return pltpu.make_async_remote_copy(
            src_ref=src.at[tile], dst_ref=dst.at[tile], send_sem=send.at[0], recv_sem=recv.at[j],
            device_id={"space": other},
        )

    cut = HEAD_DIM // 32 * 16
    halves = ((0, cut), (cut, HEAD_DIM))

    def to_frame(src, dst, tile, send, recv, j, half, target):
        r0, r1 = halves[half]
        return pltpu.make_async_remote_copy(
            src_ref=src.at[tile, r0:r1], dst_ref=dst.at[tile, r0:r1], send_sem=send.at[0], recv_sem=recv.at[half, j],
            device_id={"frame": target},
        )

    edges = [
        [
            pltpu.make_async_remote_copy(
                src_ref=src.at[pl.ds(pl.multiple_of(other * (tokens - width), width), width), lo:hi],
                dst_ref=dst.at[tokens : tokens + width, lo:hi],
                send_sem=edge_s.at[c, i], recv_sem=edge_r.at[c, i], device_id={"space": other},
            )
            for c, (src, dst) in enumerate(((q_hbm, q), (r_hbm, res)))
        ]
        for i, (lo, hi) in enumerate(zip(cuts, cuts[1:]))
    ]

    def head_of(lo, w):
        return (lax.broadcasted_iota(jnp.int32, (HEAD_DIM, w), 1) + lo) // HEAD_DIM

    def own_step(j):
        tile = 2 * j + space
        to_other(pb, rb, tile, rs_s, rs_r, j).wait_recv()
        total = st[tile] + rb[tile].astype(F32)
        st[tile] = total
        ob[tile] = total.astype(BF16)
        for half in range(2):
            to_frame(ob, yb, tile, y_s, y_r, j, half, twin).start()

    def scan_step(j, lead):
        tile = 2 * j + space
        for half, (r0, r1) in enumerate(halves):
            to_frame(ob, yb, tile, y_s, y_r, j, half, twin).wait_recv()
            beside = yb[tile, r0:r1].astype(F32)
            mine = st[tile, r0:r1]
            if lead:
                before = jnp.zeros_like(mine)
            else:
                to_frame(ps, pr, tile, z_s, z_r, j, half, frame - 2).wait_recv()
                before = pr[tile, r0:r1].astype(F32)

            @pl.when(has_next)
            def _():
                ps[tile, r0:r1] = (before + (mine + beside)).astype(BF16)
                to_frame(ps, pr, tile, z_s, z_r, j, half, frame + 2).start()

            vb[tile, r0:r1] = (before + beside * odd.astype(F32) + mine).astype(BF16)
        to_other(vb, vb, tile, pv_s, pv_r, j).start()

    ready, turned, fetched = 0, 0, 0
    for m in range(steps):
        lo, w, heads = wins[m]
        k0, k1 = HEAD_DIM * heads[0], HEAD_DIM * (heads[-1] + 1)
        while cuts[ready] < max(k1, lo + w):
            for copy in kv_loads[ready]:
                copy.wait()
            ready += 1
        while turned < k1:
            top = min(dim, turned + LANES)
            kt[turned:top, :] = jnp.maximum(k[:, turned:top], 0).T
            turned = top
        full = jnp.dot(kt[k0:k1, :], v[:, lo : lo + w], preferred_element_type=F32)
        owner = head_of(lo, w)
        slab = full[:HEAD_DIM]
        for h in heads[1:]:
            at = HEAD_DIM * h - k0
            slab = jnp.where(owner == h, full[at : at + HEAD_DIM, :], slab)
        for part in range(-(-w // LANES)):
            tile = lo // LANES + part
            wide = min(LANES, w - part * LANES)
            st[tile, :, :wide] = slab[:, part * LANES : part * LANES + wide]
            pb[tile] = st[tile].astype(BF16)
        if m == LEAD - 1:
            pl.semaphore_wait(barrier, 2 + jnp.where(has_prev, 1, 0) + jnp.where(has_next, 1, 0))
        for n in range(m + 1) if m == LEAD - 1 else range(m, m + 1) if m >= LEAD else ():
            to_other(pb, rb, 2 * n + other, rs_s, rs_r, n).start()
        if m >= LAG:
            own_step(m - LAG)
        if m >= LEAD:
            for copies in loads[fetched : fetched + 1] + edges[fetched : fetched + 1]:
                for copy in copies:
                    copy.start()
            fetched += 1
        if m >= EARLY:
            @pl.when(jnp.logical_not(has_prev))
            def _():
                scan_step(m - EARLY, True)
    for copies in loads[fetched:] + edges[fetched:]:
        for copy in copies:
            copy.start()
    for m in range(max(0, steps - LAG), steps):
        own_step(m)

    pairs = dim // PAIR

    def realign(r0, r1, j0, j1):
        for j in range(j0, min(j1, pairs)):
            qa[j, r0:r1, :PAIR] = jnp.maximum(q[r0:r1, PAIR * j : PAIR * (j + 1)], 0)
            ra[j, r0:r1, :PAIR] = res[r0:r1, PAIR * j : PAIR * (j + 1)]

    def cover(lo, hi, size):
        out = []
        while lo < hi:
            n = lo // size
            top = min(hi, size * (n + 1))
            out.append((n, lo - size * n, top - size * n))
            lo = top
        return out

    row_head = lax.broadcasted_iota(jnp.int32, (PAIR, PAIR), 0) < HEAD_DIM
    col_head = lax.broadcasted_iota(jnp.int32, (PAIR, PAIR), 1) < HEAD_DIM
    same = jnp.where(row_head == col_head, 1.0, 0.0).astype(BF16)
    first_head = lax.broadcasted_iota(jnp.int32, (HEAD_DIM, PAIR), 1) < HEAD_DIM

    def numer_step(j):
        parts = [vb[t, :, a:b] for t, a, b in cover(PAIR * j, PAIR * (j + 1), LANES)]
        slab = jnp.concatenate(parts, axis=1)
        zero = jnp.zeros_like(slab)
        both = jnp.concatenate([jnp.where(first_head, slab, zero), jnp.where(first_head, zero, slab)], axis=0)
        found = jnp.dot(qa[j, :, :PAIR], both, preferred_element_type=F32)
        numer[j % (2 * GROUP), :, :PAIR] = found
        sq[j % (2 * GROUP), :, :PAIR] = (found * found).astype(BF16)

    def mixed_step(j):
        total = jnp.dot(sq[j % (2 * GROUP), :, :PAIR], same, preferred_element_type=F32)
        scale = lax.rsqrt(total + HEAD_DIM * 1e-6)
        normed = numer[j % (2 * GROUP), :, :PAIR] * scale
        qa[j, :, :PAIR] = (ra[j, :, :PAIR].astype(F32) + normed * ga[j : j + 1, :PAIR]).astype(BF16)
        for t in range(PAIR * j // LANES, done(j + 1)):
            lo, hi = LANES * t, min(dim, LANES * (t + 1))
            parts = [qa[n, :, a:b] for n, a, b in cover(lo, hi, PAIR)]
            value = jnp.concatenate(parts, axis=1) if len(parts) > 1 else parts[0]
            mixed[width : width + tokens, lo:hi] = value[:tokens]
            mixed[far, lo:hi] = value[tokens:]

    def done(j):
        return -(-dim // LANES) if j == pairs else PAIR * j // LANES

    pitch = width + 2 * PAD
    far = pl.ds(pl.multiple_of((1 - space) * (tokens + width), width), width)
    chunk = 16

    def tree(terms):
        total = terms[0]
        for term in terms[1:]:
            total = total + term
        return total

    def conv_tile(at, keep):
        for row in range(rows + 2):
            first = row * pitch + PAD
            x32[first : first + width, :] = mixed[row * width : (row + 1) * width, at].astype(F32)
        for row in range(rows + 2):
            first = row * pitch + PAD
            here = slice(row * width, (row + 1) * width)
            left[here, :] = x32[first - 1 : first - 1 + width, :].astype(BF16)
            right[here, :] = x32[first + 1 : first + 1 + width, :].astype(BF16)
        tv, tg = ([jnp.broadcast_to(taps[f, n : n + 1, at], (chunk, LANES)).astype(BF16) for n in range(9)] for f in range(2))
        for row in range(rows):
            for off in range(0, width, chunk):
                cv = half = None
                for n in range(9):
                    start = (row + n // 3) * width + off
                    here = slice(start, start + chunk)
                    x = left[here, :] if n % 3 == 0 else mixed[here, at] if n % 3 == 1 else right[here, :]
                    cv = tv[n] * x if cv is None else cv + tv[n] * x
                    half = tg[n] * x if half is None else half + tg[n] * x
                cv, half = cv.astype(F32), half.astype(F32)
                centre = (row + 1) * pitch + PAD + off
                value = (x32[centre : centre + chunk, :] + cv * (half + half * jnp.tanh(half))).astype(BF16)
                first = row * width + off
                if keep == LANES:
                    o_ref[first : first + chunk, at] = value
                else:
                    o_ref[first : first + chunk, dim - keep : dim] = value[:, :keep]

    def conv_step(t0, t1):
        whole = min(t1, dim // LANES)

        def one(t, _):
            conv_tile(pl.ds(pl.multiple_of(t * LANES, LANES), LANES), LANES)
            return 0

        if whole > t0:
            lax.fori_loop(t0, whole, one, 0)
        if t1 > whole:
            conv_tile(slice(whole * LANES, t1 * LANES), dim - whole * LANES)

    for copy in small:
        copy.wait()
    taps[0, 0:9, 0:dim] = vt_ref[...]
    taps[1, 0:9, 0:dim] = 0.5 * gt_ref[...]
    for j in range(pairs):
        ga[j : j + 1, :PAIR] = HEAD_DIM**0.5 * gain_ref[PAIR * j : PAIR * (j + 1)].reshape(1, PAIR)

    def prepare(stage):
        if stage == 0:
            for copies in loads:
                for copy in copies:
                    copy.wait()
        if stage == stages - 1:
            for copies in edges:
                for copy in copies:
                    copy.wait_recv()
            realign(tokens, tokens + width, 0, pairs)
        realign(0, tokens, SHARE * stage, SHARE * (stage + 1))

    stages = -(-pairs // SHARE)
    deep = pair > 1

    @pl.when(deep)
    def _():
        for stage in range(stages):
            prepare(stage)

    def reach(m):
        return m + (LAST if m >= SINGLES - 1 else 1)

    starts = list(range(SINGLES)) + list(range(SINGLES, pairs, GROUP)) + [pairs]
    block = 0
    for m in range(-max(FIRST, MIDDLE, LAST, stages), steps):
        if steps - EARLY <= m + FIRST < steps:
            @pl.when(jnp.logical_not(has_prev))
            def _():
                scan_step(m + FIRST, True)

        if 0 <= m + MIDDLE < steps:
            @pl.when(jnp.logical_and(has_prev, has_next))
            def _():
                scan_step(m + MIDDLE, False)

        ahead = range(max(0, reach(m - 1) + 1), min(steps - 1, reach(m)) + 1)
        if len(ahead):
            @pl.when(jnp.logical_and(has_prev, jnp.logical_not(has_next)))
            def _():
                for n in ahead:
                    scan_step(n, False)

        if 0 <= m + stages < stages:
            @pl.when(jnp.logical_not(deep))
            def _():
                prepare(m + stages)

        if m < 0:
            continue
        to_other(vb, vb, 2 * m + other, pv_s, pv_r, m).wait_recv()
        while block + 1 < len(starts) and (PAIR * starts[block + 1] - 1) // WINDOW <= m:
            for n in range(starts[block], starts[block + 1]):
                numer_step(n)
            if block:
                for n in range(starts[block - 1], starts[block]):
                    mixed_step(n)
                conv_step(done(starts[block - 1]), done(starts[block]))
            block += 1
    for n in range(starts[-2], pairs):
        mixed_step(n)
    conv_step(done(starts[-2]), done(pairs))

    for copies in edges:
        for copy in copies:
            copy.wait_send()

    def drain(buf, send, recv, target):
        pltpu.make_async_remote_copy(
            src_ref=buf.at[0:steps], dst_ref=buf.at[0:steps], send_sem=send.at[0], recv_sem=recv, device_id=target
        ).wait_send()

    drain(pb, rs_s, rs_r.at[0], {"space": other})
    drain(ob, y_s, y_r.at[0, 0], {"frame": twin})
    drain(vb, pv_s, pv_r.at[0], {"space": other})

    @pl.when(has_next)
    def _():
        drain(ps, z_s, z_r.at[0, 0], {"frame": frame + 2})


def solution(mesh):
    frames = mesh.shape["frame"]

    def on_device(queries, keys, values, residual, attn_gain, value_taps, gate_taps):
        _, rows, width, dim = queries.shape
        tokens = rows * width
        steps = -(-dim // WINDOW)
        flat = lambda a: a.reshape(tokens, dim)
        anywhere = pl.BlockSpec(memory_space=pl.ANY)
        state = (2 * steps, HEAD_DIM, LANES)
        one, sems, split = (pltpu.SemaphoreType.DMA(n) for n in ((1,), (steps,), (2, steps)))
        pieces = pltpu.SemaphoreType.DMA((2, -(-dim // PIECE)))
        ext = tokens + width
        pairs = dim // PAIR
        across = -(-dim // LANES) * LANES
        operands = (flat(queries), flat(keys), flat(values), flat(residual), attn_gain, value_taps, gate_taps)
        out = pl.pallas_call(
            functools.partial(mix_kernel, frames, rows, width, dim),
            out_shape=jax.ShapeDtypeStruct((tokens, dim), BF16),
            in_specs=[anywhere] * 7,
            out_specs=pl.BlockSpec(memory_space=pltpu.VMEM),
            scratch_shapes=[
                pltpu.VMEM((ext, dim), BF16),
                pltpu.VMEM((tokens, dim), BF16),
                pltpu.VMEM((tokens, dim), BF16),
                pltpu.VMEM((dim, tokens), BF16),
                pltpu.VMEM((ext, dim), BF16),
                pltpu.VMEM(state, F32),
            ]
            + [pltpu.VMEM(state, BF16)] * 7
            + [
                pltpu.VMEM((pairs, ext, WINDOW), BF16),
                pltpu.VMEM((pairs, ext, WINDOW), BF16),
                pltpu.VMEM((dim,), F32),
                pltpu.VMEM((pairs, WINDOW), F32),
                pltpu.VMEM((9, dim), F32),
                pltpu.VMEM((9, dim), F32),
                pltpu.VMEM((2, 16, across), F32),
                pltpu.VMEM((2 * GROUP, ext, WINDOW), F32),
                pltpu.VMEM((2 * GROUP, ext, WINDOW), BF16),
                pltpu.VMEM((ext + width, across), BF16),
                pltpu.VMEM(((rows + 2) * (width + 2 * PAD), LANES), F32),
                pltpu.VMEM((ext + width, LANES), BF16),
                pltpu.VMEM((ext + width, LANES), BF16),
                pieces,
                pieces,
                pieces,
                pieces,
            ]
            + [one, sems, one, split, one, split, one, sems]
            + [pltpu.SemaphoreType.DMA((3,))],
            compiler_params=pltpu.CompilerParams(collective_id=0, has_side_effects=True, vmem_limit_bytes=50 << 20),
        )(*(pltpu.with_memory_space_constraint(a, pltpu.HBM) for a in operands))
        return out.reshape(1, rows, width, dim)

    placed = P(("groups", "frame"), "space", None, None)
    return jax.shard_map(
        on_device,
        mesh=mesh,
        in_specs=(placed,) * 4 + (P(),) * 3,
        out_specs=placed,
        check_vma=False,
    )
```

```python
import functools

import jax
import jax.numpy as jnp
from jax import lax
from jax.experimental import pallas as pl
from jax.experimental.pallas import tpu as pltpu
from jax.sharding import PartitionSpec as P

HEAD_DIM = 112
LANES = 128
WINDOW = 256
PAD = 8
PIECE = 384
PAIR = 2 * HEAD_DIM
LAG = 2
LEAD = 1
EARLY = 7
SHARE = 4
GROUP = 2
SINGLES = 4
FIRST, MIDDLE, LAST = 6, 4, 2
F32, BF16 = jnp.float32, jnp.bfloat16


def windows(dim):
    out = []
    for lo in range(0, dim, WINDOW):
        w = min(WINDOW, dim - lo)
        h0, h1 = lo // HEAD_DIM, (lo + w - 1) // HEAD_DIM
        out.append((lo, w, range(h0, h1 + 1)))
    return out


def mix_kernel(
    frames, rows, width, dim,
    q_hbm, k_hbm, v_hbm, r_hbm, gain_hbm, vt_hbm, gt_hbm, o_ref,
    q, k, v, kt, res, st, pb, rb, ob, yb, pr, ps, vb, qa, ra, gain_ref, ga, vt_ref, gt_ref, taps, numer, sq, mixed, x32, left, right,
    kv_sem, load_sem, edge_s, edge_r, rs_s, rs_r, y_s, y_r, z_s, z_r, pv_s, pv_r, small_sem,
):
    tokens = rows * width
    tiles = st.shape[0]
    space = lax.axis_index("space")
    frame = lax.axis_index("frame")
    other = 1 - space
    pair, odd = frame // 2, frame % 2
    twin = frame + 1 - 2 * odd
    has_prev = pair > 0
    has_next = pair < frames // 2 - 1
    wins = windows(dim)
    steps = len(wins)

    cuts = list(range(0, dim, PIECE)) + [dim]
    kv_loads = []
    for i, (lo, hi) in enumerate(zip(cuts, cuts[1:])):
        kv_loads.append(
            [
                pltpu.make_async_copy(src.at[:, lo:hi], dst.at[:, lo:hi], kv_sem.at[c, i])
                for c, (src, dst) in enumerate(((k_hbm, k), (v_hbm, v)))
            ]
        )
    loads = [
        [
            pltpu.make_async_copy(src.at[:, lo:hi], dst.at[0:tokens, lo:hi], load_sem.at[c, i])
            for c, (src, dst) in enumerate(((q_hbm, q), (r_hbm, res)))
        ]
        for i, (lo, hi) in enumerate(zip(cuts, cuts[1:]))
    ]
    for copies in kv_loads:
        for copy in copies:
            copy.start()

    small = [
        pltpu.make_async_copy(src, dst, small_sem.at[i])
        for i, (src, dst) in enumerate(((gain_hbm, gain_ref), (vt_hbm, vt_ref), (gt_hbm, gt_ref)))
    ]
    for copy in small:
        copy.start()

    barrier = pltpu.get_barrier_semaphore()
    pl.semaphore_signal(barrier, inc=1, device_id={"space": other})
    pl.semaphore_signal(barrier, inc=1, device_id={"frame": twin})

    @pl.when(has_prev)
    def _():
        pl.semaphore_signal(barrier, inc=1, device_id={"frame": frame - 2})

    @pl.when(has_next)
    def _():
        pl.semaphore_signal(barrier, inc=1, device_id={"frame": frame + 2})

    st[tiles - 1] = jnp.zeros(st.shape[1:], F32)
    x32[...] = jnp.zeros(x32.shape, F32)
    taps[...] = jnp.zeros(taps.shape, F32)
    mixed[:, dim:] = jnp.zeros((mixed.shape[0], mixed.shape[1] - dim), BF16)
    mixed[pl.ds(pl.multiple_of(space * (tokens + width), width), width), :] = jnp.zeros((width, mixed.shape[1]), BF16)

    def to_other(src, dst, tile, send, recv, j):
        return pltpu.make_async_remote_copy(
            src_ref=src.at[tile], dst_ref=dst.at[tile], send_sem=send.at[0], recv_sem=recv.at[j],
            device_id={"space": other},
        )

    cut = HEAD_DIM // 32 * 16
    halves = ((0, cut), (cut, HEAD_DIM))

    def to_frame(src, dst, tile, send, recv, j, half, target):
        r0, r1 = halves[half]
        return pltpu.make_async_remote_copy(
            src_ref=src.at[tile, r0:r1], dst_ref=dst.at[tile, r0:r1], send_sem=send.at[0], recv_sem=recv.at[half, j],
            device_id={"frame": target},
        )

    edges = [
        [
            pltpu.make_async_remote_copy(
                src_ref=src.at[pl.ds(pl.multiple_of(other * (tokens - width), width), width), lo:hi],
                dst_ref=dst.at[tokens : tokens + width, lo:hi],
                send_sem=edge_s.at[c, i], recv_sem=edge_r.at[c, i], device_id={"space": other},
            )
            for c, (src, dst) in enumerate(((q_hbm, q), (r_hbm, res)))
        ]
        for i, (lo, hi) in enumerate(zip(cuts, cuts[1:]))
    ]

    def head_of(lo, w):
        return (lax.broadcasted_iota(jnp.int32, (HEAD_DIM, w), 1) + lo) // HEAD_DIM

    def own_step(j):
        tile = 2 * j + space
        to_other(pb, rb, tile, rs_s, rs_r, j).wait_recv()
        total = st[tile] + rb[tile].astype(F32)
        st[tile] = total
        ob[tile] = total.astype(BF16)
        for half in range(2):
            to_frame(ob, yb, tile, y_s, y_r, j, half, twin).start()

    def scan_step(j, lead):
        tile = 2 * j + space
        for half, (r0, r1) in enumerate(halves):
            to_frame(ob, yb, tile, y_s, y_r, j, half, twin).wait_recv()
            beside = yb[tile, r0:r1].astype(F32)
            mine = st[tile, r0:r1]
            if lead:
                before = jnp.zeros_like(mine)
            else:
                to_frame(ps, pr, tile, z_s, z_r, j, half, frame - 2).wait_recv()
                before = pr[tile, r0:r1].astype(F32)

            @pl.when(has_next)
            def _():
                ps[tile, r0:r1] = (before + (mine + beside)).astype(BF16)
                to_frame(ps, pr, tile, z_s, z_r, j, half, frame + 2).start()

            vb[tile, r0:r1] = (before + beside * odd.astype(F32) + mine).astype(BF16)
        to_other(vb, vb, tile, pv_s, pv_r, j).start()

    ready, turned, fetched = 0, 0, 0
    for m in range(steps):
        lo, w, heads = wins[m]
        k0, k1 = HEAD_DIM * heads[0], HEAD_DIM * (heads[-1] + 1)
        while cuts[ready] < max(k1, lo + w):
            for copy in kv_loads[ready]:
                copy.wait()
            ready += 1
        while turned < k1:
            top = min(dim, turned + LANES)
            kt[turned:top, :] = jnp.maximum(k[:, turned:top], 0).T
            turned = top
        full = jnp.dot(kt[k0:k1, :], v[:, lo : lo + w], preferred_element_type=F32)
        owner = head_of(lo, w)
        slab = full[:HEAD_DIM]
        for h in heads[1:]:
            at = HEAD_DIM * h - k0
            slab = jnp.where(owner == h, full[at : at + HEAD_DIM, :], slab)
        for part in range(-(-w // LANES)):
            tile = lo // LANES + part
            wide = min(LANES, w - part * LANES)
            st[tile, :, :wide] = slab[:, part * LANES : part * LANES + wide]
            pb[tile] = st[tile].astype(BF16)
        if m == LEAD - 1:
            pl.semaphore_wait(barrier, 2 + jnp.where(has_prev, 1, 0) + jnp.where(has_next, 1, 0))
        for n in range(m + 1) if m == LEAD - 1 else range(m, m + 1) if m >= LEAD else ():
            to_other(pb, rb, 2 * n + other, rs_s, rs_r, n).start()
        if m >= LAG:
            own_step(m - LAG)
        if m >= LEAD:
            for copies in loads[fetched : fetched + 1] + edges[fetched : fetched + 1]:
                for copy in copies:
                    copy.start()
            fetched += 1
        if m >= EARLY:
            @pl.when(jnp.logical_not(has_prev))
            def _():
                scan_step(m - EARLY, True)
    for copies in loads[fetched:] + edges[fetched:]:
        for copy in copies:
            copy.start()
    for m in range(max(0, steps - LAG), steps):
        own_step(m)

    pairs = dim // PAIR

    def realign(r0, r1, j0, j1):
        for j in range(j0, min(j1, pairs)):
            qa[j, r0:r1, :PAIR] = jnp.maximum(q[r0:r1, PAIR * j : PAIR * (j + 1)], 0)
            ra[j, r0:r1, :PAIR] = res[r0:r1, PAIR * j : PAIR * (j + 1)]

    def cover(lo, hi, size):
        out = []
        while lo < hi:
            n = lo // size
            top = min(hi, size * (n + 1))
            out.append((n, lo - size * n, top - size * n))
            lo = top
        return out

    row_head = lax.broadcasted_iota(jnp.int32, (PAIR, PAIR), 0) < HEAD_DIM
    col_head = lax.broadcasted_iota(jnp.int32, (PAIR, PAIR), 1) < HEAD_DIM
    same = jnp.where(row_head == col_head, 1.0, 0.0).astype(BF16)
    first_head = lax.broadcasted_iota(jnp.int32, (HEAD_DIM, PAIR), 1) < HEAD_DIM

    def numer_step(j):
        parts = [vb[t, :, a:b] for t, a, b in cover(PAIR * j, PAIR * (j + 1), LANES)]
        slab = jnp.concatenate(parts, axis=1)
        zero = jnp.zeros_like(slab)
        both = jnp.concatenate([jnp.where(first_head, slab, zero), jnp.where(first_head, zero, slab)], axis=0)
        found = jnp.dot(qa[j, :, :PAIR], both, preferred_element_type=F32)
        numer[j % (2 * GROUP), :, :PAIR] = found
        sq[j % (2 * GROUP), :, :PAIR] = (found * found).astype(BF16)

    def mixed_step(j):
        total = jnp.dot(sq[j % (2 * GROUP), :, :PAIR], same, preferred_element_type=F32)
        scale = lax.rsqrt(total + HEAD_DIM * 1e-6)
        normed = numer[j % (2 * GROUP), :, :PAIR] * scale
        qa[j, :, :PAIR] = (ra[j, :, :PAIR].astype(F32) + normed * ga[j : j + 1, :PAIR]).astype(BF16)
        for t in range(PAIR * j // LANES, done(j + 1)):
            lo, hi = LANES * t, min(dim, LANES * (t + 1))
            parts = [qa[n, :, a:b] for n, a, b in cover(lo, hi, PAIR)]
            value = jnp.concatenate(parts, axis=1) if len(parts) > 1 else parts[0]
            mixed[width : width + tokens, lo:hi] = value[:tokens]
            mixed[far, lo:hi] = value[tokens:]

    def done(j):
        return -(-dim // LANES) if j == pairs else PAIR * j // LANES

    pitch = width + 2 * PAD
    far = pl.ds(pl.multiple_of((1 - space) * (tokens + width), width), width)
    chunk = 16

    def tree(terms):
        total = terms[0]
        for term in terms[1:]:
            total = total + term
        return total

    def conv_tile(at, keep):
        for row in range(rows + 2):
            first = row * pitch + PAD
            x32[first : first + width, :] = mixed[row * width : (row + 1) * width, at].astype(F32)
        for row in range(rows + 2):
            first = row * pitch + PAD
            here = slice(row * width, (row + 1) * width)
            left[here, :] = x32[first - 1 : first - 1 + width, :].astype(BF16)
            right[here, :] = x32[first + 1 : first + 1 + width, :].astype(BF16)
        tv, tg = ([jnp.broadcast_to(taps[f, n : n + 1, at], (chunk, LANES)).astype(BF16) for n in range(9)] for f in range(2))
        for row in range(rows):
            for off in range(0, width, chunk):
                cv = half = None
                for n in range(9):
                    start = (row + n // 3) * width + off
                    here = slice(start, start + chunk)
                    x = left[here, :] if n % 3 == 0 else mixed[here, at] if n % 3 == 1 else right[here, :]
                    cv = tv[n] * x if cv is None else cv + tv[n] * x
                    half = tg[n] * x if half is None else half + tg[n] * x
                cv, half = cv.astype(F32), half.astype(F32)
                centre = (row + 1) * pitch + PAD + off
                value = (x32[centre : centre + chunk, :] + cv * (half + half * jnp.tanh(half))).astype(BF16)
                first = row * width + off
                if keep == LANES:
                    o_ref[first : first + chunk, at] = value
                else:
                    o_ref[first : first + chunk, dim - keep : dim] = value[:, :keep]

    def conv_step(t0, t1):
        whole = min(t1, dim // LANES)

        def one(t, _):
            conv_tile(pl.ds(pl.multiple_of(t * LANES, LANES), LANES), LANES)
            return 0

        if whole > t0:
            lax.fori_loop(t0, whole, one, 0)
        if t1 > whole:
            conv_tile(slice(whole * LANES, t1 * LANES), dim - whole * LANES)

    for copy in small:
        copy.wait()
    taps[0, 0:9, 0:dim] = vt_ref[...]
    taps[1, 0:9, 0:dim] = 0.5 * gt_ref[...]
    for j in range(pairs):
        ga[j : j + 1, :PAIR] = HEAD_DIM**0.5 * gain_ref[PAIR * j : PAIR * (j + 1)].reshape(1, PAIR)

    def prepare(stage):
        if stage == 0:
            for copies in loads:
                for copy in copies:
                    copy.wait()
        if stage == stages - 1:
            for copies in edges:
                for copy in copies:
                    copy.wait_recv()
            realign(tokens, tokens + width, 0, pairs)
        realign(0, tokens, SHARE * stage, SHARE * (stage + 1))

    stages = -(-pairs // SHARE)
    deep = pair > 1

    @pl.when(deep)
    def _():
        for stage in range(stages):
            prepare(stage)

    def reach(m):
        return m + (LAST if m >= SINGLES - 1 else 1)

    starts = list(range(SINGLES)) + list(range(SINGLES, pairs, GROUP)) + [pairs]
    block = 0
    for m in range(-max(FIRST, MIDDLE, LAST, stages), steps):
        if steps - EARLY <= m + FIRST < steps:
            @pl.when(jnp.logical_not(has_prev))
            def _():
                scan_step(m + FIRST, True)

        if 0 <= m + MIDDLE < steps:
            @pl.when(jnp.logical_and(has_prev, has_next))
            def _():
                scan_step(m + MIDDLE, False)

        ahead = range(max(0, reach(m - 1) + 1), min(steps - 1, reach(m)) + 1)
        if len(ahead):
            @pl.when(jnp.logical_and(has_prev, jnp.logical_not(has_next)))
            def _():
                for n in ahead:
                    scan_step(n, False)

        if 0 <= m + stages < stages:
            @pl.when(jnp.logical_not(deep))
            def _():
                prepare(m + stages)

        if m < 0:
            continue
        to_other(vb, vb, 2 * m + other, pv_s, pv_r, m).wait_recv()
        while block + 1 < len(starts) and (PAIR * starts[block + 1] - 1) // WINDOW <= m:
            if block:
                for n in range(starts[block - 1], starts[block]):
                    mixed_step(n)
            for n in range(starts[block], starts[block + 1]):
                numer_step(n)
            if block:
                conv_step(done(starts[block - 1]), done(starts[block]))
            block += 1
    for n in range(starts[-2], pairs):
        mixed_step(n)
    conv_step(done(starts[-2]), done(pairs))

    for copies in edges:
        for copy in copies:
            copy.wait_send()

    def drain(buf, send, recv, target):
        pltpu.make_async_remote_copy(
            src_ref=buf.at[0:steps], dst_ref=buf.at[0:steps], send_sem=send.at[0], recv_sem=recv, device_id=target
        ).wait_send()

    drain(pb, rs_s, rs_r.at[0], {"space": other})
    drain(ob, y_s, y_r.at[0, 0], {"frame": twin})
    drain(vb, pv_s, pv_r.at[0], {"space": other})

    @pl.when(has_next)
    def _():
        drain(ps, z_s, z_r.at[0, 0], {"frame": frame + 2})


def solution(mesh):
    frames = mesh.shape["frame"]

    def on_device(queries, keys, values, residual, attn_gain, value_taps, gate_taps):
        _, rows, width, dim = queries.shape
        tokens = rows * width
        steps = -(-dim // WINDOW)
        flat = lambda a: a.reshape(tokens, dim)
        anywhere = pl.BlockSpec(memory_space=pl.ANY)
        state = (2 * steps, HEAD_DIM, LANES)
        one, sems, split = (pltpu.SemaphoreType.DMA(n) for n in ((1,), (steps,), (2, steps)))
        pieces = pltpu.SemaphoreType.DMA((2, -(-dim // PIECE)))
        ext = tokens + width
        pairs = dim // PAIR
        across = -(-dim // LANES) * LANES
        operands = (flat(queries), flat(keys), flat(values), flat(residual), attn_gain, value_taps, gate_taps)
        out = pl.pallas_call(
            functools.partial(mix_kernel, frames, rows, width, dim),
            out_shape=jax.ShapeDtypeStruct((tokens, dim), BF16),
            in_specs=[anywhere] * 7,
            out_specs=pl.BlockSpec(memory_space=pltpu.VMEM),
            scratch_shapes=[
                pltpu.VMEM((ext, dim), BF16),
                pltpu.VMEM((tokens, dim), BF16),
                pltpu.VMEM((tokens, dim), BF16),
                pltpu.VMEM((dim, tokens), BF16),
                pltpu.VMEM((ext, dim), BF16),
                pltpu.VMEM(state, F32),
            ]
            + [pltpu.VMEM(state, BF16)] * 7
            + [
                pltpu.VMEM((pairs, ext, WINDOW), BF16),
                pltpu.VMEM((pairs, ext, WINDOW), BF16),
                pltpu.VMEM((dim,), F32),
                pltpu.VMEM((pairs, WINDOW), F32),
                pltpu.VMEM((9, dim), F32),
                pltpu.VMEM((9, dim), F32),
                pltpu.VMEM((2, 16, across), F32),
                pltpu.VMEM((2 * GROUP, ext, WINDOW), F32),
                pltpu.VMEM((2 * GROUP, ext, WINDOW), BF16),
                pltpu.VMEM((ext + width, across), BF16),
                pltpu.VMEM(((rows + 2) * (width + 2 * PAD), LANES), F32),
                pltpu.VMEM((ext + width, LANES), BF16),
                pltpu.VMEM((ext + width, LANES), BF16),
                pieces,
                pieces,
                pieces,
                pieces,
            ]
            + [one, sems, one, split, one, split, one, sems]
            + [pltpu.SemaphoreType.DMA((3,))],
            compiler_params=pltpu.CompilerParams(collective_id=0, has_side_effects=True, vmem_limit_bytes=50 << 20),
        )(*(pltpu.with_memory_space_constraint(a, pltpu.HBM) for a in operands))
        return out.reshape(1, rows, width, dim)

    placed = P(("groups", "frame"), "space", None, None)
    return jax.shard_map(
        on_device,
        mesh=mesh,
        in_specs=(placed,) * 4 + (P(),) * 3,
        out_specs=placed,
        check_vma=False,
    )
```

```python
import functools

import jax
import jax.numpy as jnp
from jax import lax
from jax.experimental import pallas as pl
from jax.experimental.pallas import tpu as pltpu
from jax.sharding import PartitionSpec as P

HEAD_DIM = 112
LANES = 128
WINDOW = 256
PAD = 8
PIECE = 384
PAIR = 2 * HEAD_DIM
LAG = 2
LEAD = 1
EARLY = 7
SHARE = 4
GROUP = 2
SINGLES = 4
FIRST, MIDDLE, LAST = 6, 4, 2
F32, BF16 = jnp.float32, jnp.bfloat16


def windows(dim):
    out = []
    for lo in range(0, dim, WINDOW):
        w = min(WINDOW, dim - lo)
        h0, h1 = lo // HEAD_DIM, (lo + w - 1) // HEAD_DIM
        out.append((lo, w, range(h0, h1 + 1)))
    return out


def mix_kernel(
    frames, rows, width, dim,
    q_hbm, k_hbm, v_hbm, r_hbm, gain_hbm, vt_hbm, gt_hbm, o_ref,
    q, k, v, kt, res, st, pb, rb, ob, yb, pr, ps, vb, qa, ra, gain_ref, ga, vt_ref, gt_ref, taps, numer, sq, mixed, x32, left, right,
    kv_sem, load_sem, edge_s, edge_r, rs_s, rs_r, y_s, y_r, z_s, z_r, pv_s, pv_r, small_sem,
):
    tokens = rows * width
    tiles = st.shape[0]
    space = lax.axis_index("space")
    frame = lax.axis_index("frame")
    other = 1 - space
    pair, odd = frame // 2, frame % 2
    twin = frame + 1 - 2 * odd
    has_prev = pair > 0
    has_next = pair < frames // 2 - 1
    wins = windows(dim)
    steps = len(wins)

    cuts = list(range(0, dim, PIECE)) + [dim]
    kv_loads = []
    for i, (lo, hi) in enumerate(zip(cuts, cuts[1:])):
        kv_loads.append(
            [
                pltpu.make_async_copy(src.at[:, lo:hi], dst.at[:, lo:hi], kv_sem.at[c, i])
                for c, (src, dst) in enumerate(((k_hbm, k), (v_hbm, v)))
            ]
        )
    loads = [
        [
            pltpu.make_async_copy(src.at[:, lo:hi], dst.at[0:tokens, lo:hi], load_sem.at[c, i])
            for c, (src, dst) in enumerate(((q_hbm, q), (r_hbm, res)))
        ]
        for i, (lo, hi) in enumerate(zip(cuts, cuts[1:]))
    ]
    for copies in kv_loads:
        for copy in copies:
            copy.start()

    small = [
        pltpu.make_async_copy(src, dst, small_sem.at[i])
        for i, (src, dst) in enumerate(((gain_hbm, gain_ref), (vt_hbm, vt_ref), (gt_hbm, gt_ref)))
    ]
    for copy in small:
        copy.start()

    barrier = pltpu.get_barrier_semaphore()
    pl.semaphore_signal(barrier, inc=1, device_id={"space": other})
    pl.semaphore_signal(barrier, inc=1, device_id={"frame": twin})

    @pl.when(has_prev)
    def _():
        pl.semaphore_signal(barrier, inc=1, device_id={"frame": frame - 2})

    @pl.when(has_next)
    def _():
        pl.semaphore_signal(barrier, inc=1, device_id={"frame": frame + 2})

    st[tiles - 1] = jnp.zeros(st.shape[1:], F32)
    x32[...] = jnp.zeros(x32.shape, F32)
    taps[...] = jnp.zeros(taps.shape, F32)
    mixed[:, dim:] = jnp.zeros((mixed.shape[0], mixed.shape[1] - dim), BF16)
    mixed[pl.ds(pl.multiple_of(space * (tokens + width), width), width), :] = jnp.zeros((width, mixed.shape[1]), BF16)

    def to_other(src, dst, tile, send, recv, j):
        return pltpu.make_async_remote_copy(
            src_ref=src.at[tile], dst_ref=dst.at[tile], send_sem=send.at[0], recv_sem=recv.at[j],
            device_id={"space": other},
        )

    cut = HEAD_DIM // 32 * 16
    halves = ((0, cut), (cut, HEAD_DIM))

    def to_frame(src, dst, tile, send, recv, j, half, target):
        r0, r1 = halves[half]
        return pltpu.make_async_remote_copy(
            src_ref=src.at[tile, r0:r1], dst_ref=dst.at[tile, r0:r1], send_sem=send.at[0], recv_sem=recv.at[half, j],
            device_id={"frame": target},
        )

    edges = [
        [
            pltpu.make_async_remote_copy(
                src_ref=src.at[pl.ds(pl.multiple_of(other * (tokens - width), width), width), lo:hi],
                dst_ref=dst.at[tokens : tokens + width, lo:hi],
                send_sem=edge_s.at[c, i], recv_sem=edge_r.at[c, i], device_id={"space": other},
            )
            for c, (src, dst) in enumerate(((q_hbm, q), (r_hbm, res)))
        ]
        for i, (lo, hi) in enumerate(zip(cuts, cuts[1:]))
    ]

    def head_of(lo, w):
        return (lax.broadcasted_iota(jnp.int32, (HEAD_DIM, w), 1) + lo) // HEAD_DIM

    def own_step(j):
        tile = 2 * j + space
        to_other(pb, rb, tile, rs_s, rs_r, j).wait_recv()
        total = st[tile] + rb[tile].astype(F32)
        st[tile] = total
        ob[tile] = total.astype(BF16)
        for half in range(2):
            to_frame(ob, yb, tile, y_s, y_r, j, half, twin).start()

    def scan_step(j, lead):
        tile = 2 * j + space
        for half, (r0, r1) in enumerate(halves):
            to_frame(ob, yb, tile, y_s, y_r, j, half, twin).wait_recv()
            beside = yb[tile, r0:r1].astype(F32)
            mine = st[tile, r0:r1]
            if lead:
                before = jnp.zeros_like(mine)
            else:
                to_frame(ps, pr, tile, z_s, z_r, j, half, frame - 2).wait_recv()
                before = pr[tile, r0:r1].astype(F32)

            @pl.when(has_next)
            def _():
                ps[tile, r0:r1] = (before + (mine + beside)).astype(BF16)
                to_frame(ps, pr, tile, z_s, z_r, j, half, frame + 2).start()

            vb[tile, r0:r1] = (before + beside * odd.astype(F32) + mine).astype(BF16)
        to_other(vb, vb, tile, pv_s, pv_r, j).start()

    ready, turned, fetched = 0, 0, 0
    for m in range(steps):
        lo, w, heads = wins[m]
        k0, k1 = HEAD_DIM * heads[0], HEAD_DIM * (heads[-1] + 1)
        while cuts[ready] < max(k1, lo + w):
            for copy in kv_loads[ready]:
                copy.wait()
            ready += 1
        while turned < k1:
            top = min(dim, turned + LANES)
            kt[turned:top, :] = jnp.maximum(k[:, turned:top], 0).T
            turned = top
        full = jnp.dot(kt[k0:k1, :], v[:, lo : lo + w], preferred_element_type=F32)
        owner = head_of(lo, w)
        slab = full[:HEAD_DIM]
        for h in heads[1:]:
            at = HEAD_DIM * h - k0
            slab = jnp.where(owner == h, full[at : at + HEAD_DIM, :], slab)
        for part in range(-(-w // LANES)):
            tile = lo // LANES + part
            wide = min(LANES, w - part * LANES)
            st[tile, :, :wide] = slab[:, part * LANES : part * LANES + wide]
            pb[tile] = st[tile].astype(BF16)
        if m == LEAD - 1:
            pl.semaphore_wait(barrier, 2 + jnp.where(has_prev, 1, 0) + jnp.where(has_next, 1, 0))
        for n in range(m + 1) if m == LEAD - 1 else range(m, m + 1) if m >= LEAD else ():
            to_other(pb, rb, 2 * n + other, rs_s, rs_r, n).start()
        if m >= LAG:
            own_step(m - LAG)
        if m >= LEAD:
            for copies in loads[fetched : fetched + 1] + edges[fetched : fetched + 1]:
                for copy in copies:
                    copy.start()
            fetched += 1
        if m >= EARLY:
            @pl.when(jnp.logical_not(has_prev))
            def _():
                scan_step(m - EARLY, True)
    for copies in loads[fetched:] + edges[fetched:]:
        for copy in copies:
            copy.start()
    for m in range(max(0, steps - LAG), steps):
        own_step(m)

    pairs = dim // PAIR

    def realign(r0, r1, j0, j1):
        for j in range(j0, min(j1, pairs)):
            qa[j, r0:r1, :PAIR] = jnp.maximum(q[r0:r1, PAIR * j : PAIR * (j + 1)], 0)
            ra[j, r0:r1, :PAIR] = res[r0:r1, PAIR * j : PAIR * (j + 1)]

    def cover(lo, hi, size):
        out = []
        while lo < hi:
            n = lo // size
            top = min(hi, size * (n + 1))
            out.append((n, lo - size * n, top - size * n))
            lo = top
        return out

    row_head = lax.broadcasted_iota(jnp.int32, (PAIR, PAIR), 0) < HEAD_DIM
    col_head = lax.broadcasted_iota(jnp.int32, (PAIR, PAIR), 1) < HEAD_DIM
    same = jnp.where(row_head == col_head, 1.0, 0.0).astype(BF16)
    first_head = lax.broadcasted_iota(jnp.int32, (HEAD_DIM, PAIR), 1) < HEAD_DIM

    def numer_step(j):
        parts = [vb[t, :, a:b] for t, a, b in cover(PAIR * j, PAIR * (j + 1), LANES)]
        slab = jnp.concatenate(parts, axis=1)
        zero = jnp.zeros_like(slab)
        both = jnp.concatenate([jnp.where(first_head, slab, zero), jnp.where(first_head, zero, slab)], axis=0)
        found = jnp.dot(qa[j, :, :PAIR], both, preferred_element_type=F32)
        numer[j % (2 * GROUP), :, :PAIR] = found
        near = found.astype(BF16)
        sq[j % (2 * GROUP), :, :PAIR] = near * near

    def mixed_step(j):
        total = jnp.dot(sq[j % (2 * GROUP), :, :PAIR], same, preferred_element_type=F32)
        scale = lax.rsqrt(total + HEAD_DIM * 1e-6)
        normed = numer[j % (2 * GROUP), :, :PAIR] * scale
        qa[j, :, :PAIR] = (ra[j, :, :PAIR].astype(F32) + normed * ga[j : j + 1, :PAIR]).astype(BF16)
        for t in range(PAIR * j // LANES, done(j + 1)):
            lo, hi = LANES * t, min(dim, LANES * (t + 1))
            parts = [qa[n, :, a:b] for n, a, b in cover(lo, hi, PAIR)]
            value = jnp.concatenate(parts, axis=1) if len(parts) > 1 else parts[0]
            mixed[width : width + tokens, lo:hi] = value[:tokens]
            mixed[far, lo:hi] = value[tokens:]

    def done(j):
        return -(-dim // LANES) if j == pairs else PAIR * j // LANES

    pitch = width + 2 * PAD
    far = pl.ds(pl.multiple_of((1 - space) * (tokens + width), width), width)
    chunk = 16

    def tree(terms):
        total = terms[0]
        for term in terms[1:]:
            total = total + term
        return total

    def conv_tile(at, keep):
        for row in range(rows + 2):
            first = row * pitch + PAD
            x32[first : first + width, :] = mixed[row * width : (row + 1) * width, at].astype(F32)
        for row in range(rows + 2):
            first = row * pitch + PAD
            here = slice(row * width, (row + 1) * width)
            left[here, :] = x32[first - 1 : first - 1 + width, :].astype(BF16)
            right[here, :] = x32[first + 1 : first + 1 + width, :].astype(BF16)
        tv, tg = ([jnp.broadcast_to(taps[f, n : n + 1, at], (chunk, LANES)).astype(BF16) for n in range(9)] for f in range(2))
        for row in range(rows):
            for off in range(0, width, chunk):
                cv = half = None
                for n in range(9):
                    start = (row + n // 3) * width + off
                    here = slice(start, start + chunk)
                    x = left[here, :] if n % 3 == 0 else mixed[here, at] if n % 3 == 1 else right[here, :]
                    cv = tv[n] * x if cv is None else cv + tv[n] * x
                    half = tg[n] * x if half is None else half + tg[n] * x
                cv, half = cv.astype(F32), half.astype(F32)
                centre = (row + 1) * pitch + PAD + off
                value = (x32[centre : centre + chunk, :] + cv * (half + half * jnp.tanh(half))).astype(BF16)
                first = row * width + off
                if keep == LANES:
                    o_ref[first : first + chunk, at] = value
                else:
                    o_ref[first : first + chunk, dim - keep : dim] = value[:, :keep]

    def conv_step(t0, t1):
        whole = min(t1, dim // LANES)

        def one(t, _):
            conv_tile(pl.ds(pl.multiple_of(t * LANES, LANES), LANES), LANES)
            return 0

        if whole > t0:
            lax.fori_loop(t0, whole, one, 0)
        if t1 > whole:
            conv_tile(slice(whole * LANES, t1 * LANES), dim - whole * LANES)

    for copy in small:
        copy.wait()
    taps[0, 0:9, 0:dim] = vt_ref[...]
    taps[1, 0:9, 0:dim] = 0.5 * gt_ref[...]
    for j in range(pairs):
        ga[j : j + 1, :PAIR] = HEAD_DIM**0.5 * gain_ref[PAIR * j : PAIR * (j + 1)].reshape(1, PAIR)

    def prepare(stage):
        if stage == 0:
            for copies in loads:
                for copy in copies:
                    copy.wait()
        if stage == stages - 1:
            for copies in edges:
                for copy in copies:
                    copy.wait_recv()
            realign(tokens, tokens + width, 0, pairs)
        realign(0, tokens, SHARE * stage, SHARE * (stage + 1))

    stages = -(-pairs // SHARE)
    deep = pair > 1

    @pl.when(deep)
    def _():
        for stage in range(stages):
            prepare(stage)

    def reach(m):
        return m + (LAST if m >= SINGLES - 1 else 1)

    starts = list(range(SINGLES)) + list(range(SINGLES, pairs, GROUP)) + [pairs]
    block = 0
    for m in range(-max(FIRST, MIDDLE, LAST, stages), steps):
        if steps - EARLY <= m + FIRST < steps:
            @pl.when(jnp.logical_not(has_prev))
            def _():
                scan_step(m + FIRST, True)

        if 0 <= m + MIDDLE < steps:
            @pl.when(jnp.logical_and(has_prev, has_next))
            def _():
                scan_step(m + MIDDLE, False)

        ahead = range(max(0, reach(m - 1) + 1), min(steps - 1, reach(m)) + 1)
        if len(ahead):
            @pl.when(jnp.logical_and(has_prev, jnp.logical_not(has_next)))
            def _():
                for n in ahead:
                    scan_step(n, False)

        if 0 <= m + stages < stages:
            @pl.when(jnp.logical_not(deep))
            def _():
                prepare(m + stages)

        if m < 0:
            continue
        to_other(vb, vb, 2 * m + other, pv_s, pv_r, m).wait_recv()
        while block + 1 < len(starts) and (PAIR * starts[block + 1] - 1) // WINDOW <= m:
            if block:
                for n in range(starts[block - 1], starts[block]):
                    mixed_step(n)
            for n in range(starts[block], starts[block + 1]):
                numer_step(n)
            if block:
                conv_step(done(starts[block - 1]), done(starts[block]))
            block += 1
    for n in range(starts[-2], pairs):
        mixed_step(n)
    conv_step(done(starts[-2]), done(pairs))

    for copies in edges:
        for copy in copies:
            copy.wait_send()

    def drain(buf, send, recv, target):
        pltpu.make_async_remote_copy(
            src_ref=buf.at[0:steps], dst_ref=buf.at[0:steps], send_sem=send.at[0], recv_sem=recv, device_id=target
        ).wait_send()

    drain(pb, rs_s, rs_r.at[0], {"space": other})
    drain(ob, y_s, y_r.at[0, 0], {"frame": twin})
    drain(vb, pv_s, pv_r.at[0], {"space": other})

    @pl.when(has_next)
    def _():
        drain(ps, z_s, z_r.at[0, 0], {"frame": frame + 2})


def solution(mesh):
    frames = mesh.shape["frame"]

    def on_device(queries, keys, values, residual, attn_gain, value_taps, gate_taps):
        _, rows, width, dim = queries.shape
        tokens = rows * width
        steps = -(-dim // WINDOW)
        flat = lambda a: a.reshape(tokens, dim)
        anywhere = pl.BlockSpec(memory_space=pl.ANY)
        state = (2 * steps, HEAD_DIM, LANES)
        one, sems, split = (pltpu.SemaphoreType.DMA(n) for n in ((1,), (steps,), (2, steps)))
        pieces = pltpu.SemaphoreType.DMA((2, -(-dim // PIECE)))
        ext = tokens + width
        pairs = dim // PAIR
        across = -(-dim // LANES) * LANES
        operands = (flat(queries), flat(keys), flat(values), flat(residual), attn_gain, value_taps, gate_taps)
        out = pl.pallas_call(
            functools.partial(mix_kernel, frames, rows, width, dim),
            out_shape=jax.ShapeDtypeStruct((tokens, dim), BF16),
            in_specs=[anywhere] * 7,
            out_specs=pl.BlockSpec(memory_space=pltpu.VMEM),
            scratch_shapes=[
                pltpu.VMEM((ext, dim), BF16),
                pltpu.VMEM((tokens, dim), BF16),
                pltpu.VMEM((tokens, dim), BF16),
                pltpu.VMEM((dim, tokens), BF16),
                pltpu.VMEM((ext, dim), BF16),
                pltpu.VMEM(state, F32),
            ]
            + [pltpu.VMEM(state, BF16)] * 7
            + [
                pltpu.VMEM((pairs, ext, WINDOW), BF16),
                pltpu.VMEM((pairs, ext, WINDOW), BF16),
                pltpu.VMEM((dim,), F32),
                pltpu.VMEM((pairs, WINDOW), F32),
                pltpu.VMEM((9, dim), F32),
                pltpu.VMEM((9, dim), F32),
                pltpu.VMEM((2, 16, across), F32),
                pltpu.VMEM((2 * GROUP, ext, WINDOW), F32),
                pltpu.VMEM((2 * GROUP, ext, WINDOW), BF16),
                pltpu.VMEM((ext + width, across), BF16),
                pltpu.VMEM(((rows + 2) * (width + 2 * PAD), LANES), F32),
                pltpu.VMEM((ext + width, LANES), BF16),
                pltpu.VMEM((ext + width, LANES), BF16),
                pieces,
                pieces,
                pieces,
                pieces,
            ]
            + [one, sems, one, split, one, split, one, sems]
            + [pltpu.SemaphoreType.DMA((3,))],
            compiler_params=pltpu.CompilerParams(collective_id=0, has_side_effects=True, vmem_limit_bytes=50 << 20),
        )(*(pltpu.with_memory_space_constraint(a, pltpu.HBM) for a in operands))
        return out.reshape(1, rows, width, dim)

    placed = P(("groups", "frame"), "space", None, None)
    return jax.shard_map(
        on_device,
        mesh=mesh,
        in_specs=(placed,) * 4 + (P(),) * 3,
        out_specs=placed,
        check_vma=False,
    )
```
